32 devices in a mesh: dp: 8 (over z, x), tensor: 4 (over y, core).
Axes of the slice: x: 2, y: 2, z: 4, core: 2. Of those that a mesh axis runs over, the one named last changes fastest.
Arguments:
- tokens_in: bfloat16 [16384, 1536], P('dp'), may hold values from -6 to 6
- segments: int32 [16384], P('dp'), may hold values from 0 to 63, never falling along the last dimension, each value on 1 to 1024 neighbouring positions
- pre_gain: float32 [1536], replicated, may hold values from 0.5 to 1.5
- gate_proj: bfloat16 [1536, 3072], P(None, 'tensor'), may hold values from -0.15625 to 0.15625
- value_proj: bfloat16 [1536, 3072], P(None, 'tensor'), may hold values from -0.15625 to 0.15625
- state_proj: bfloat16 [1536, 256], replicated, may hold values from -0.15625 to 0.15625
- step_proj: bfloat16 [1536, 48], P(None, 'tensor'), may hold values from -0.15625 to 0.15625
- conv_value: float32 [4, 3072], P(None, 'tensor'), may hold values from -3 to 3
- conv_value_bias: float32 [3072], P('tensor'), may hold values from -0.5 to 0.5
- conv_state: float32 [4, 256], replicated, may hold values from -3 to 3
- conv_state_bias: float32 [256], replicated, may hold values from -0.5 to 0.5
- step_bias: float32 [48], P('tensor'), may hold values from -6.9 to -2.25
- decay_log: float32 [48], P('tensor'), may hold values from 0 to 2.77
- skip_gain: float32 [48], P('tensor'), may hold values from 0.5 to 1.5
- norm_gain: float32 [3072], P('tensor'), may hold values from 0.5 to 1.5
- out_proj: bfloat16 [3072, 1536], P('tensor'), may hold values from -0.109375 to 0.109375
- grad_out: bfloat16 [16384, 1536], P('dp'), may hold values from -6 to 6
Outputs:
- block_out: bfloat16 [16384, 1536], P('dp')
- grad_in: bfloat16 [16384, 1536], P('dp')
- grad_pre_gain: float32 [1536], replicated
- grad_gate_proj: float32 [1536, 3072], P(None, 'tensor')
- grad_value_proj: float32 [1536, 3072], P(None, 'tensor')
- grad_state_proj: float32 [1536, 256], replicated
- grad_step_proj: float32 [1536, 48], P(None, 'tensor')
- grad_conv_value: float32 [4, 3072], P(None, 'tensor')
- grad_conv_value_bias: float32 [3072], P('tensor')
- grad_conv_state: float32 [4, 256], replicated
- grad_conv_state_bias: float32 [256], replicated
- grad_step_bias: float32 [48], P('tensor')
- grad_decay_log: float32 [48], P('tensor')
- grad_skip_gain: float32 [48], P('tensor')
- grad_norm_gain: float32 [3072], P('tensor')
- grad_out_proj: float32 [3072, 1536], P('tensor')
The draws below stay inside these ranges and needn't reach their ends.
Inputs may be any that keep to these rules, and one draw needn't show every extreme that they name: `segments`: segment numbers never fall along the tokens.
All inputs are finite; a program needn't handle non-finite values.
Results may differ from the reference program's by a relative error of at most 0.018.
Values may be sent and summed in bfloat16 or wider, within the bound.
No kernel may reach another device: no remote copies, remote signals or barrier semaphores. Data moves between devices by JAX's collectives and lax.ppermute only.
A program may use at most 256 MiB of HBM per device.

```python
import math
import jax
import jax.numpy as jnp
import numpy as np
from jax import lax

D = 1536
H = 48
N = 128
K = 4
D_INNER = 3072
SEQ_LEN = 1024
TOKENS = 16384
N_TENSOR = 4


def levels(rng, shape, split, least, top_value):
    level = 1.0
    for dim, blocks in split:
        draws = jax.random.uniform(jax.random.fold_in(jax.random.fold_in(rng, 6), dim), (blocks,), jnp.float32, least / len(split), top_value / len(split))
        level = level * jnp.repeat(jnp.exp(draws), shape[dim] // blocks).reshape((-1,) + (1,) * (len(shape) - 1 - dim))
    return level


def length_profile(amount, total, limit, slope):
    weights = [(1 << 20) // math.isqrt(rank ** slope) + 1 for rank in range(2, amount + 1)]
    spare, given = total - limit - (amount - 1), [1] * (amount - 1)
    while spare > 0:
        movable = [i for i in range(amount - 1) if given[i] < limit]
        mass, budget = sum([weights[i] for i in movable]), spare
        for i in movable:
            extra = min(limit - given[i], max(1, budget * weights[i] // mass), spare)
            given[i] = given[i] + extra
            spare = spare - extra
    return np.array([limit] + given)


def uneven(rng, amount, total, reach, lean):
    if amount == 2:
        one = jax.random.randint(rng, (), max(1, total - reach), min(reach, total - 1) + 1)
        return jnp.stack([one, total - one])
    lengths = jnp.asarray(length_profile(amount, total, reach, lean), jnp.int32)
    pairs = (amount - 1) // 2
    source_of, taker = lengths[1:1 + 2 * pairs:2], lengths[2:2 + 2 * pairs:2]
    slack = jnp.minimum(source_of - 1, reach - taker)
    moved = jax.random.randint(jax.random.fold_in(rng, 1), (pairs,), 0, 1 << 20) % (slack + 1)
    lengths = lengths.at[1:1 + 2 * pairs:2].set(source_of - moved).at[2:2 + 2 * pairs:2].set(taker + moved)
    return lengths[jax.random.permutation(jax.random.fold_in(rng, 2), amount)]


def gaussian(key, dims, width, reach, split=(), held_as=jnp.bfloat16):
    result = width * jax.random.normal(key, dims, jnp.float32)
    if split:
        result = result * levels(key, dims, split, -0.22, 0.18)
    return jnp.clip(result, -reach, reach).astype(held_as)


def setup_inputs(seed: int = 0) -> dict:
    splits = jax.random.split(jax.random.key(seed), 18)
    tokens_in = gaussian(splits[0], (TOKENS, D), 1.0, 6.0, ((0, 8),))
    segments = jnp.searchsorted(jnp.cumsum(uneven(splits[1], TOKENS // (SEQ_LEN // 4), TOKENS, SEQ_LEN, 2)), jnp.arange(TOKENS), side="right").astype(jnp.int32)
    pre_gain = jnp.clip(1.0 + 0.1 * jax.random.normal(splits[2], (D,), jnp.float32), 0.5, 1.5)
    gate_proj = gaussian(splits[3], (D, D_INNER), D ** -0.5, 0.15625, ((1, 4),))
    value_proj = gaussian(splits[4], (D, D_INNER), D ** -0.5, 0.15625, ((1, 4),))
    state_proj = gaussian(splits[5], (D, 2 * N), D ** -0.5, 0.15625)
    step_proj = gaussian(splits[6], (D, H), D ** -0.5, 0.15625, ((1, 4),))
    conv_value = gaussian(splits[7], (K, D_INNER), K ** -0.5, 3.0, ((1, 4),), jnp.float32)
    conv_value_bias = jnp.clip(jax.random.uniform(splits[8], (D_INNER,), jnp.float32, -0.5, 0.5) * levels(splits[8], (D_INNER,), ((0, 4),), -0.4, 0.0), -0.5, 0.5)
    conv_state = gaussian(splits[9], (K, 2 * N), K ** -0.5, 3.0, (), jnp.float32)
    conv_state_bias = jnp.clip(jax.random.uniform(splits[10], (2 * N,), jnp.float32, -0.5, 0.5), -0.5, 0.5)
    step_bias = jnp.clip(-6.9 + 4.65 * jax.random.uniform(splits[11], (H,), jnp.float32) ** levels(splits[11], (H,), ((0, 4),), -0.2, 0.2), -6.9, -2.25)
    decay_log = jnp.clip(2.77 * jax.random.uniform(splits[12], (H,), jnp.float32) ** levels(splits[12], (H,), ((0, 4),), -0.2, 0.2), 0.0, 2.77)
    skip_gain = jnp.clip(0.5 + 1.0 * jax.random.uniform(splits[13], (H,), jnp.float32) ** levels(splits[13], (H,), ((0, 4),), -0.2, 0.2), 0.5, 1.5)
    norm_gain = jnp.clip(1.0 + 0.1 * jax.random.normal(splits[14], (D_INNER,), jnp.float32), 0.5, 1.5)
    out_proj = gaussian(splits[15], (D_INNER, D), D_INNER ** -0.5, 0.109375, ((0, 4),))
    grad_out = gaussian(splits[16], (TOKENS, D), 1.0, 6.0, ((0, 8),))
    return {"tokens_in": tokens_in, "segments": segments, "pre_gain": pre_gain, "gate_proj": gate_proj, "value_proj": value_proj, "state_proj": state_proj, "step_proj": step_proj, "conv_value": conv_value, "conv_value_bias": conv_value_bias, "conv_state": conv_state, "conv_state_bias": conv_state_bias, "step_bias": step_bias, "decay_log": decay_log, "skip_gain": skip_gain, "norm_gain": norm_gain, "out_proj": out_proj, "grad_out": grad_out}


eps_value = 1e-05
precise = lax.Precision.HIGHEST

def shifted(values, offset):
    padding = jnp.zeros((offset,) + values.shape[1:], values.dtype)
    return jnp.concatenate([padding, values[:-offset]], axis=0)

def lifted(values, offset):
    padding = jnp.zeros((offset,) + values.shape[1:], values.dtype)
    return jnp.concatenate([values[offset:], padding], axis=0)

def conv_masks(segments):
    position = jnp.arange(segments.shape[0], dtype=jnp.int32) % SEQ_LEN
    masks = []
    for offset in range(1, K):
        keep_mask = (position >= offset) & (segments == shifted(segments, offset))
        masks.append(keep_mask.astype(jnp.float32)[:, None])
    return masks

def conv_forward(raw_rows, kernel_taps, shift_bias, masks):
    running = shift_bias + kernel_taps[K - 1] * raw_rows
    for offset in range(1, K):
        running = running + kernel_taps[K - 1 - offset] * shifted(raw_rows, offset) * masks[offset - 1]
    return running

def conv_backward(raw_rows, grad_pre, kernel_taps, masks):
    grad_raw = kernel_taps[K - 1] * grad_pre
    tap_grads = [lax.optimization_barrier(jnp.sum(grad_pre * raw_rows, axis=0))]
    for offset in range(1, K):
        masked = grad_pre * masks[offset - 1]
        grad_raw = grad_raw + kernel_taps[K - 1 - offset] * lifted(masked, offset)
        tap_grads.append(lax.optimization_barrier(jnp.sum(masked * shifted(raw_rows, offset), axis=0)))
    return (grad_raw, jnp.stack(tap_grads[::-1], axis=0), lax.optimization_barrier(jnp.sum(grad_pre, axis=0)))

def silu_slope(values):
    logistic = jax.nn.sigmoid(values)
    return logistic * (1.0 + values * (1.0 - logistic))

def tile_terms(c_rows, b_cols, cum_rows, cum_cols, step_cols, seg_rows, seg_cols, row_start, col_start):
    scores = jnp.dot(c_rows, b_cols.T, preferred_element_type=jnp.float32)
    span_size = c_rows.shape[0]
    row_pos = row_start + jnp.arange(span_size, dtype=jnp.int32)
    col_pos = col_start + jnp.arange(span_size, dtype=jnp.int32)
    causal = (seg_rows[:, None] == seg_cols[None, :]) & (row_pos[:, None] >= col_pos[None, :])
    log_decay = cum_rows[:, :, None] - cum_cols[:, None, :]
    kernel = jnp.where(causal[None], jnp.exp(jnp.minimum(log_decay, 0.0)), 0.0)
    weights = kernel * step_cols[:, None, :]
    mixing = (scores[None] * weights).astype(jnp.bfloat16)
    return (scores, kernel, weights, mixing)

def ssd_forward(value_bf, value_act, b_mat, c_mat, step_size, seg_rows, decay_rate, skip_gain):
    seq_length = value_bf.shape[0]
    head_count = step_size.shape[1]
    head_width = value_bf.shape[1] // head_count
    span_size = min(512, seq_length)
    span_count = seq_length // span_size
    cum_heads = jnp.cumsum(step_size * decay_rate[None, :], axis=0).T
    step_heads = step_size.T
    value_heads = value_bf.reshape(seq_length, head_count, head_width).astype(jnp.float32)
    pieces = []
    for row_blk in range(span_count):
        row_lo = row_blk * span_size
        row_hi = row_lo + span_size
        running = jnp.zeros((span_size, head_count, head_width), jnp.float32)
        for col_blk in range(row_blk + 1):
            col_lo = col_blk * span_size
            col_hi = col_lo + span_size
            scores, kernel, weights, mixing = tile_terms(c_mat[row_lo:row_hi], b_mat[col_lo:col_hi], cum_heads[:, row_lo:row_hi], cum_heads[:, col_lo:col_hi], step_heads[:, col_lo:col_hi], seg_rows[row_lo:row_hi], seg_rows[col_lo:col_hi], row_lo, col_lo)
            running = running + jnp.einsum('hqs,shp->qhp', mixing.astype(jnp.float32), value_heads[col_lo:col_hi], precision=precise)
        pieces.append(running)
    ssd_out = jnp.concatenate(pieces, axis=0).reshape(seq_length, head_count * head_width)
    return ssd_out + jnp.repeat(skip_gain, head_width)[None, :] * value_act

def ssd_backward(value_bf, value_act, b_mat, c_mat, step_size, seg_rows, decay_rate, skip_gain, grad_mix):
    seq_length = value_bf.shape[0]
    head_count = step_size.shape[1]
    head_width = value_bf.shape[1] // head_count
    state_size = b_mat.shape[1]
    span_size = min(512, seq_length)
    span_count = seq_length // span_size
    cum_heads = jnp.cumsum(step_size * decay_rate[None, :], axis=0).T
    step_heads = step_size.T
    value_heads = value_bf.reshape(seq_length, head_count, head_width).astype(jnp.float32)
    grad_heads = grad_mix.astype(jnp.bfloat16).reshape(seq_length, head_count, head_width).astype(jnp.float32)
    grad_value = [jnp.zeros((span_size, head_count, head_width), jnp.float32) for blk_idx in range(span_count)]
    grad_b = [jnp.zeros((span_size, state_size), jnp.float32) for blk_idx in range(span_count)]
    grad_c = [jnp.zeros((span_size, state_size), jnp.float32) for blk_idx in range(span_count)]
    row_energy = [jnp.zeros((head_count, span_size), jnp.float32) for blk_idx in range(span_count)]
    col_energy = [jnp.zeros((head_count, span_size), jnp.float32) for blk_idx in range(span_count)]
    grad_step = [jnp.zeros((head_count, span_size), jnp.float32) for blk_idx in range(span_count)]
    for row_blk in range(span_count):
        row_lo = row_blk * span_size
        row_hi = row_lo + span_size
        for col_blk in range(row_blk + 1):
            col_lo = col_blk * span_size
            col_hi = col_lo + span_size
            scores, kernel, weights, mixing = tile_terms(c_mat[row_lo:row_hi], b_mat[col_lo:col_hi], cum_heads[:, row_lo:row_hi], cum_heads[:, col_lo:col_hi], step_heads[:, col_lo:col_hi], seg_rows[row_lo:row_hi], seg_rows[col_lo:col_hi], row_lo, col_lo)
            grad_mixing = jnp.einsum('qhp,shp->hqs', grad_heads[row_lo:row_hi], value_heads[col_lo:col_hi], precision=precise)
            grad_value[col_blk] = grad_value[col_blk] + jnp.einsum('hqs,qhp->shp', mixing.astype(jnp.float32), grad_heads[row_lo:row_hi], precision=precise)
            grad_weights = grad_mixing * scores[None]
            grad_scores = lax.optimization_barrier(jnp.sum(grad_mixing * weights, axis=0))
            grad_c[row_blk] = grad_c[row_blk] + jnp.dot(grad_scores, b_mat[col_lo:col_hi].astype(jnp.float32), precision=precise)
            grad_b[col_blk] = grad_b[col_blk] + jnp.dot(grad_scores.T, c_mat[row_lo:row_hi].astype(jnp.float32), precision=precise)
            energy = grad_weights * weights
            row_energy[row_blk] = row_energy[row_blk] + lax.optimization_barrier(jnp.sum(energy, axis=2))
            col_energy[col_blk] = col_energy[col_blk] + lax.optimization_barrier(jnp.sum(energy, axis=1))
            grad_step[col_blk] = grad_step[col_blk] + lax.optimization_barrier(jnp.sum(grad_weights * kernel, axis=1))
    grad_cum = jnp.concatenate(row_energy, axis=1) - jnp.concatenate(col_energy, axis=1)
    grad_acc = lax.cumsum(grad_cum, axis=1, reverse=True)
    grad_step_all = jnp.concatenate(grad_step, axis=1) + grad_acc * decay_rate[:, None]
    grad_decay = lax.optimization_barrier(jnp.sum(grad_acc * step_heads, axis=1))
    grad_skip = lax.optimization_barrier(jnp.sum((grad_mix * value_act).reshape(seq_length, head_count, head_width), axis=(0, 2)))
    grad_value_all = jnp.concatenate(grad_value, axis=0).reshape(seq_length, head_count * head_width)
    grad_value_all = grad_value_all + jnp.repeat(skip_gain, head_width)[None, :] * grad_mix
    return (grad_value_all, jnp.concatenate(grad_b, axis=0), jnp.concatenate(grad_c, axis=0), grad_step_all.T, grad_decay, grad_skip)

def sequence_pass(params, tok_rows, seg_rows, grad_rows):
    pre_gain, gate_proj, value_proj, state_proj, step_proj, conv_value, conv_value_bias, conv_state, conv_state_bias, step_bias, decay_log, skip_gain, norm_gain, out_proj = params
    hidden = tok_rows.astype(jnp.float32)
    inv_rms = lax.rsqrt(lax.optimization_barrier(jnp.mean(hidden * hidden, axis=1, keepdims=True)) + eps_value)
    normed = (hidden * inv_rms * pre_gain).astype(jnp.bfloat16)
    masks = conv_masks(seg_rows)
    state_raw = jnp.dot(normed, state_proj, preferred_element_type=jnp.float32)
    state_pre = conv_forward(state_raw, conv_state, conv_state_bias, masks)
    state_act = jax.nn.silu(state_pre).astype(jnp.bfloat16)
    b_mat = state_act[:, :N]
    c_mat = state_act[:, N:]
    group_width = D_INNER // N_TENSOR
    group_heads = H // N_TENSOR
    saved = []
    squares = jnp.zeros((tok_rows.shape[0],), jnp.float32)
    for group_idx in range(N_TENSOR):
        channels = slice(group_idx * group_width, (group_idx + 1) * group_width)
        head_sel = slice(group_idx * group_heads, (group_idx + 1) * group_heads)
        gate_raw = jnp.dot(normed, gate_proj[:, channels], preferred_element_type=jnp.float32)
        value_raw = jnp.dot(normed, value_proj[:, channels], preferred_element_type=jnp.float32)
        step_raw = jnp.dot(normed, step_proj[:, head_sel], preferred_element_type=jnp.float32)
        value_pre = conv_forward(value_raw, conv_value[:, channels], conv_value_bias[channels], masks)
        value_act = jax.nn.silu(value_pre)
        value_bf = value_act.astype(jnp.bfloat16)
        step_size = jax.nn.softplus(step_raw + step_bias[head_sel])
        decay_rate = -jnp.exp(decay_log[head_sel])
        ssd_out = ssd_forward(value_bf, value_act, b_mat, c_mat, step_size, seg_rows, decay_rate, skip_gain[head_sel])
        gated_y = ssd_out * jax.nn.silu(gate_raw)
        squares = squares + lax.optimization_barrier(jnp.sum(gated_y * gated_y, axis=1))
        saved.append((gate_raw, value_raw, step_raw, value_pre, value_act, value_bf, step_size, decay_rate, ssd_out, gated_y))
    gate_scale = lax.rsqrt(squares[:, None] / D_INNER + eps_value)
    branch = jnp.zeros(hidden.shape, jnp.float32)
    inner_sum = jnp.zeros((tok_rows.shape[0],), jnp.float32)
    norm_parts = []
    out_grads = []
    norm_grads = []
    for group_idx in range(N_TENSOR):
        channels = slice(group_idx * group_width, (group_idx + 1) * group_width)
        gated_y = saved[group_idx][9]
        unit_rows = gated_y * gate_scale
        normed_out = (unit_rows * norm_gain[channels]).astype(jnp.bfloat16)
        group_out = jnp.dot(normed_out, out_proj[channels, :], preferred_element_type=jnp.float32).astype(jnp.bfloat16)
        branch = branch + lax.optimization_barrier(group_out).astype(jnp.float32)
        grad_normed_out = jnp.dot(grad_rows, out_proj[channels, :].T, preferred_element_type=jnp.float32)
        out_grads.append(jnp.dot(normed_out.T, grad_rows, preferred_element_type=jnp.float32))
        norm_grads.append(lax.optimization_barrier(jnp.sum(grad_normed_out * unit_rows, axis=0)))
        grad_unit = grad_normed_out * norm_gain[channels]
        inner_sum = inner_sum + lax.optimization_barrier(jnp.sum(grad_unit * unit_rows, axis=1))
        norm_parts.append((unit_rows, grad_unit))
    block_out = (hidden + branch).astype(jnp.bfloat16)
    grad_normed = jnp.zeros(hidden.shape, jnp.float32)
    gate_grads = []
    value_grads = []
    step_grads = []
    conv_value_grads = []
    conv_bias_grads = []
    step_bias_grads = []
    decay_grads = []
    skip_grads = []
    state_proj_grad = jnp.zeros(state_proj.shape, jnp.float32)
    conv_state_grad = jnp.zeros(conv_state.shape, jnp.float32)
    conv_state_bias_grad = jnp.zeros(conv_state_bias.shape, jnp.float32)
    for group_idx in range(N_TENSOR):
        channels = slice(group_idx * group_width, (group_idx + 1) * group_width)
        head_sel = slice(group_idx * group_heads, (group_idx + 1) * group_heads)
        gate_raw, value_raw, step_raw, value_pre, value_act, value_bf, step_size, decay_rate, ssd_out, gated_y = saved[group_idx]
        unit_rows, grad_unit = norm_parts[group_idx]
        grad_gated = gate_scale * (grad_unit - unit_rows * inner_sum[:, None] / D_INNER)
        logistic = jax.nn.sigmoid(gate_raw)
        grad_mix = grad_gated * gate_raw * logistic
        grad_gate = grad_gated * ssd_out * logistic * (1.0 + gate_raw * (1.0 - logistic))
        grad_value, grad_b, grad_c, grad_step, grad_decay, grad_skip = ssd_backward(value_bf, value_act, b_mat, c_mat, step_size, seg_rows, decay_rate, skip_gain[head_sel], grad_mix)
        grad_value_pre = grad_value * silu_slope(value_pre)
        grad_value_raw, tap_value, bias_value = conv_backward(value_raw, grad_value_pre, conv_value[:, channels], masks)
        grad_state_pre = jnp.concatenate([grad_b, grad_c], axis=1) * silu_slope(state_pre)
        grad_state_raw, tap_state, bias_state = conv_backward(state_raw, grad_state_pre, conv_state, masks)
        grad_step_raw = grad_step * jax.nn.sigmoid(step_raw + step_bias[head_sel])
        gate_bf = grad_gate.astype(jnp.bfloat16)
        value_grad_bf = grad_value_raw.astype(jnp.bfloat16)
        step_grad_bf = grad_step_raw.astype(jnp.bfloat16)
        group_in = jnp.dot(gate_bf, gate_proj[:, channels].T, preferred_element_type=jnp.float32)
        group_in = group_in + jnp.dot(value_grad_bf, value_proj[:, channels].T, preferred_element_type=jnp.float32)
        group_in = group_in + jnp.dot(step_grad_bf, step_proj[:, head_sel].T, preferred_element_type=jnp.float32)
        group_in = group_in + jnp.dot(grad_state_raw, state_proj.astype(jnp.float32).T, precision=precise)
        grad_normed = grad_normed + lax.optimization_barrier(group_in.astype(jnp.bfloat16)).astype(jnp.float32)
        gate_grads.append(jnp.dot(normed.T, gate_bf, preferred_element_type=jnp.float32))
        value_grads.append(jnp.dot(normed.T, value_grad_bf, preferred_element_type=jnp.float32))
        step_grads.append(jnp.dot(normed.T, step_grad_bf, preferred_element_type=jnp.float32))
        state_proj_grad = state_proj_grad + jnp.dot(normed.astype(jnp.float32).T, grad_state_raw, precision=precise)
        conv_value_grads.append(tap_value)
        conv_bias_grads.append(bias_value)
        conv_state_grad = conv_state_grad + tap_state
        conv_state_bias_grad = conv_state_bias_grad + bias_state
        step_bias_grads.append(lax.optimization_barrier(jnp.sum(grad_step_raw, axis=0)))
        decay_grads.append(grad_decay * decay_rate)
        skip_grads.append(grad_skip)
    weighted = pre_gain * grad_normed
    grad_pre_gain = lax.optimization_barrier(jnp.sum(grad_normed * hidden * inv_rms, axis=0))
    grad_hidden = inv_rms * weighted - hidden * (inv_rms * inv_rms * inv_rms) * lax.optimization_barrier(jnp.mean(weighted * hidden, axis=1, keepdims=True))
    grad_in = (grad_rows.astype(jnp.float32) + grad_hidden).astype(jnp.bfloat16)
    grads = (grad_pre_gain, jnp.concatenate(gate_grads, axis=1), jnp.concatenate(value_grads, axis=1), state_proj_grad, jnp.concatenate(step_grads, axis=1), jnp.concatenate(conv_value_grads, axis=1), jnp.concatenate(conv_bias_grads, axis=0), conv_state_grad, conv_state_bias_grad, jnp.concatenate(step_bias_grads, axis=0), jnp.concatenate(decay_grads, axis=0), jnp.concatenate(skip_grads, axis=0), jnp.concatenate(norm_grads, axis=0), jnp.concatenate(out_grads, axis=0))
    return (block_out, grad_in, grads)

def reference(tokens_in, segments, pre_gain, gate_proj, value_proj, state_proj, step_proj, conv_value, conv_value_bias, conv_state, conv_state_bias, step_bias, decay_log, skip_gain, norm_gain, out_proj, grad_out):
    params = (pre_gain, gate_proj, value_proj, state_proj, step_proj, conv_value, conv_value_bias, conv_state, conv_state_bias, step_bias, decay_log, skip_gain, norm_gain, out_proj)
    seq_count = tokens_in.shape[0] // SEQ_LEN
    stacked = (tokens_in.reshape(seq_count, SEQ_LEN, D), segments.reshape(seq_count, SEQ_LEN), grad_out.reshape(seq_count, SEQ_LEN, D))
    initial = tuple((jnp.zeros(parameter.shape, jnp.float32) for parameter in params))

    def advance(carry, members):
        block_out, grad_in, grads = sequence_pass(params, members[0], members[1], members[2])
        return (tuple((carried + added for carried, added in zip(carry, grads))), (block_out, grad_in))
    totals, (outs_all, grads_in) = lax.scan(advance, initial, stacked)
    return (outs_all.reshape(seq_count * SEQ_LEN, D), grads_in.reshape(seq_count * SEQ_LEN, D), totals[0], totals[1], totals[2], totals[3], totals[4], totals[5], totals[6], totals[7], totals[8], totals[9], totals[10], totals[11], totals[12], totals[13])
```

```python
import math

import jax
import jax.numpy as jnp
import numpy as np
from jax import lax
from jax.experimental import pallas as pl
from jax.experimental.pallas import tpu as pltpu
from jax.sharding import PartitionSpec as P


N = 128
K = 4
SEQ_LEN = 1024
T = 128
LANES = 128
HALF = 64
NEG = -1e30
eps_value = 1e-05
f32 = jnp.float32
bf16 = jnp.bfloat16


def dot(a, b):
    return jnp.dot(a, b, preferred_element_type=f32)


def dot_nt(a, b):
    return lax.dot_general(a, b, (((1,), (1,)), ((), ())), preferred_element_type=f32)


def dot_tn(a, b):
    return lax.dot_general(a, b, (((0,), (0,)), ((), ())), preferred_element_type=f32)


def sigmoid(v):
    return 0.5 * jnp.tanh(0.5 * v) + 0.5


def two_terms(v):
    high = v.astype(bf16)
    return high, (v - high.astype(f32)).astype(bf16)


def paired(v):
    high, low = two_terms(v)
    lane = lax.broadcasted_iota(jnp.int32, v.shape, 1)
    return jnp.where(lane < HALF, high, low)


def sum_rows(v):
    total = v[0:8]
    for row in range(8, v.shape[0], 8):
        total = total + v[row : row + 8]
    return total


def head_rows(heads_ref, lane_ref):
    count = heads_ref.shape[1]
    lane_ref[...] = jnp.zeros_like(lane_ref)
    lane_ref[0:2, 0:count] = heads_ref[...]
    lane_ref[0:2, HALF : HALF + count] = heads_ref[...]
    return lane_ref[0:1, :], -jnp.exp(lane_ref[1:2, :])


def head_terms(z_ref, bias, rate, aux, tri_ref, e_ref, ex_ref):
    z = z_ref[...] + bias
    tail = jnp.exp(-jnp.abs(z))
    step = jnp.maximum(z, 0.0) + jnp.log1p(tail)
    high, low = two_terms(step * rate)
    cum = dot(tri_ref[...], high) + dot(tri_ref[...], low)
    end = cum[T - 1 : T]
    dst = jnp.exp(cum) * aux[:, 3:4]
    dend = jnp.exp(end - cum) * aux[:, 4:5]
    total = jnp.exp(jnp.broadcast_to(end, (8, LANES))) * aux[T - 1 : T, 3:4]
    stacked = jnp.concatenate([paired(step), paired(dend), paired(dst)], axis=0)
    ex_ref[...] = dot(stacked, e_ref[...])
    carry = dot(paired(total), e_ref[...])[0:1]
    return z, step, cum, cum.T, carry


def taps_of(c, width, vtaps_ref, staps_ref):
    ref, at = (vtaps_ref, c) if c.start < width else (staps_ref, slice(c.start - width, c.stop - width))
    return lambda s: ref[K - 1 - s : K - s, at]


def lead_kernel(
    tokens_ref, go_ref, aux_ref, pg_ref, gate_w, value_w, state_w, step_w, out_w,
    vtaps_ref, staps_ref, vbias_ref, sbias_ref, heads_ref, skip_ref, ng_ref, e_ref, tri_ref,
    normed_ref, gate_ref, vs_ref, z_ref, gno_ref, y_ref, act_ref, pre_ref, stat_ref, sin_ref,
    ext_ref, state_ref, ex_ref, sum_ref, lane_ref,
):
    rows, width = gate_ref.shape
    chunks = range(rows // T)

    @pl.when(pl.program_id(0) % (SEQ_LEN // rows) == 0)
    def _():
        state_ref[...] = jnp.zeros_like(state_ref)
        ext_ref[0:8, :] = jnp.zeros_like(ext_ref[0:8, :])

    part = 32
    for lo in range(0, rows, part):
        hidden = tokens_ref[lo : lo + part, :].astype(f32)
        inv = lax.rsqrt(jnp.mean(hidden * hidden, axis=1, keepdims=True) + eps_value)
        for k in range(pg_ref.shape[0]):
            c = slice(k * LANES, (k + 1) * LANES)
            normed_ref[lo : lo + part, c] = (hidden[:, c] * inv * pg_ref[k : k + 1, :]).astype(bf16)
    z = dot_nt(normed_ref[...], step_w[...])
    z_ref[...] = jnp.zeros_like(z_ref)
    z_ref[:, : z.shape[1]] = z
    z_ref[:, HALF : HALF + z.shape[1]] = z
    raw = dot(normed_ref[...], state_w[...])
    ext_ref[8:, width:] = raw
    vs_ref[:, width:] = raw.astype(bf16)
    at = [pl.ds(k * T, T) for k in chunks]
    bias, rate = head_rows(heads_ref, lane_ref)
    aux = [aux_ref[k].T for k in chunks]
    terms = [
        head_terms(z_ref.at[at[k]], bias, rate, aux[k], tri_ref, e_ref, ex_ref.at[k])
        for k in chunks
    ]
    keep = [
        [jnp.broadcast_to(aux[k][:, s : s + 1], (T, LANES)) for s in range(K - 1)] for k in chunks
    ]

    def activate(c, k):
        lo = 8 + k * T
        tap, shift = taps_of(c, width, vtaps_ref, staps_ref), c.start // LANES
        if c.start < width:
            pre = vbias_ref[shift : shift + 1, :]
        else:
            pre = sbias_ref[shift - width // LANES : shift - width // LANES + 1, :]
        pre = pre + tap(0) * ext_ref[lo : lo + T, c]
        for s in range(1, K):
            pre = pre + tap(s) * (ext_ref[lo - s : lo - s + T, c] * keep[k][s - 1])
        half = 0.5 * pre
        act = half + half * jnp.tanh(half)
        act_bf = act.astype(bf16)
        pre_ref[at[k], c] = pre.astype(bf16)
        act_ref[at[k], c] = act_bf
        return act, act_bf

    row = lax.broadcasted_iota(jnp.int32, (T, T), 0)
    col = lax.broadcasted_iota(jnp.int32, (T, T), 1)
    b_flip, c_mats, scores, fades = [], [], [], []
    for k in chunks:
        _, b_mat = activate(slice(width, width + N), k)
        _, c_mat = activate(slice(width + N, width + 2 * N), k)
        b_flip.append(b_mat.T)
        c_mats.append(c_mat)
        scores.append(dot_nt(c_mat, b_mat))
        same = (aux[k][:, 5:6] == aux_ref[k, 5:6, :]) & (row >= col)
        fades.append(jnp.where(same, 0.0, NEG))
    first = lax.broadcasted_iota(jnp.int32, (T, LANES), 1) < HALF
    sum_ref[...] = jnp.zeros_like(sum_ref)
    span = 2 * LANES if width % (2 * LANES) == 0 else LANES
    for lo in range(0, width, span):
        group = slice(lo, lo + span)
        raw = dot(normed_ref[...], value_w[:, group])
        ext_ref[8:, group] = raw
        vs_ref[:, group] = raw.astype(bf16)
        gates = dot(normed_ref[...], gate_w[:, group])
        gate_ref[:, group] = gates.astype(bf16)
        gnos = dot_nt(go_ref[...], out_w[group, :])
        gno_ref[:, group] = gnos.astype(bf16)
        for pair in range(lo // LANES, (lo + span) // LANES):
            c = slice(pair * LANES, (pair + 1) * LANES)
            inside = slice(pair * LANES - lo, (pair + 1) * LANES - lo)
            for k in chunks:
                _, _, cum, cum_t, carry = terms[k]
                r = slice(k * T, (k + 1) * T)
                act, act_bf = activate(c, k)
                xt_full = act_bf.astype(f32) * ex_ref[k, 0:T, c]
                xt = xt_full.astype(bf16)
                xd = (xt_full * ex_ref[k, T : 2 * T, c]).astype(bf16)
                mixes = []
                for h in (2 * pair, 2 * pair + 1):
                    decay = jnp.exp(fades[k] + (cum[:, h : h + 1] - cum_t[h : h + 1, :]))
                    mixes.append((scores[k] * decay).astype(bf16))
                zero = jnp.zeros_like(xt)
                blocks = [jnp.where(first, xt, zero), jnp.where(first, zero, xt)]
                state = state_ref[:, c]
                state_bf = state.astype(bf16)
                sin_ref[k, :, c] = state_bf
                y = dot(jnp.concatenate(mixes, axis=1), jnp.concatenate(blocks, axis=0))
                y = y + ex_ref[k, 2 * T : 3 * T, c] * dot(c_mats[k], state_bf)
                y_ref[r, c] = y
                state_ref[:, c] = state * carry[:, c] + dot(b_flip[k], xd)
                half = 0.5 * gates[r, inside]
                gated = (y + skip_ref[pair : pair + 1, :] * act) * (half + half * jnp.tanh(half))
                sum_ref[k, 0] += gated * gated
                sum_ref[k, 1] += gated * ng_ref[pair : pair + 1, :] * gnos[r, inside]
    for k in chunks:
        for s in range(2):
            stat_ref[k, s : s + 1, :] = jnp.sum(sum_ref[k, s].T, axis=0, keepdims=True)
    ext_ref[0:8, :] = ext_ref[rows : rows + 8, :]


def store_half(value, sent_ref, kept_ref):
    first = pl.program_id(0) < pl.num_programs(0) // 2

    @pl.when(first)
    def _():
        sent_ref[...] = value

    @pl.when(jnp.logical_not(first))
    def _():
        kept_ref[...] = value


def middle_kernel(
    _, gate_ref, gno_ref, y_ref, act_ref, stat_ref, skip_ref, ng_ref, out_w,
    gate_grad_ref, mix_ref, normed_ref, sent_ref, kept_ref, csum_ref,
):
    @pl.when(pl.program_id(0) == 0)
    def _():
        csum_ref[...] = jnp.zeros_like(csum_ref)

    for chunk in range(stat_ref.shape[0]):
        r = slice(chunk * T, (chunk + 1) * T)
        scale = jnp.broadcast_to(stat_ref[chunk, 0:1, :], (LANES, T)).T
        slope_scale = jnp.broadcast_to(stat_ref[chunk, 1:2, :], (LANES, T)).T
        for pair in range(gate_ref.shape[1] // LANES):
            c = slice(pair * LANES, (pair + 1) * LANES)
            gate = gate_ref[r, c].astype(f32)
            logistic = sigmoid(gate)
            swish = gate * logistic
            x = act_ref[r, c].astype(f32)
            gno = gno_ref[r, c].astype(f32)
            ssd = y_ref[r, c] + skip_ref[pair : pair + 1, :] * x
            gated = ssd * swish
            unit = gated * scale
            normed_ref[r, c] = (unit * ng_ref[pair : pair + 1, :]).astype(bf16)
            grad_gated = scale * (gno * ng_ref[pair : pair + 1, :]) - slope_scale * gated
            csum_ref[0:8, c] += sum_rows(gno * unit)
            grad_mix = grad_gated * swish
            grad_gate = grad_gated * ssd * (logistic + swish * (1.0 - logistic))
            gate_grad_ref[r, c] = grad_gate.astype(bf16)
            csum_ref[8:16, c] += sum_rows(grad_mix * x)
            mix_ref[r, c] = grad_mix.astype(bf16)

    store_half(dot(normed_ref[...], out_w[...]).astype(bf16), sent_ref, kept_ref)


def backward_kernel(
    mix_ref, y_ref, act_ref, pre_ref, vs_ref, z_ref, sin_ref, aux_ref,
    vtaps_ref, staps_ref, heads_ref, skip_ref, e_ref, er_ref, tri_ref, triu_ref,
    grad_ref, csum_ref,
    back_ref, ext_ref, ex_ref, xd_ref, gd_ref, through_ref, lane_ref, part_ref,
):
    width = mix_ref.shape[1]

    @pl.when((pl.program_id(0) == 0) & (pl.program_id(1) == 0))
    def _():
        csum_ref[...] = jnp.zeros_like(csum_ref)

    @pl.when(pl.program_id(1) == 0)
    def _():
        back_ref[...] = jnp.zeros_like(back_ref)
        ext_ref[T : T + 8, :] = jnp.zeros_like(ext_ref[T : T + 8, :])

    bias, rate = head_rows(heads_ref, lane_ref)
    aux = aux_ref[0].T
    z, step, cum, cum_t, carry = head_terms(z_ref, bias, rate, aux, tri_ref, e_ref, ex_ref)
    keep = [jnp.broadcast_to(aux[:, 5 + s : 6 + s], (T, LANES)) for s in range(1, K)]
    b_mat = act_ref[:, width : width + N]
    c_mat = act_ref[:, width + N : width + 2 * N]
    scores_t = dot_nt(b_mat, c_mat)
    row = lax.broadcasted_iota(jnp.int32, (T, T), 0)
    col = lax.broadcasted_iota(jnp.int32, (T, T), 1)
    same = (aux[:, 5:6] == aux_ref[0, 5:6, :]) & (row <= col)
    fade = jnp.where(same, 0.0, NEG)
    lane = lax.broadcasted_iota(jnp.int32, (T, LANES), 1)
    first = lane < HALF
    back_bf = back_ref[...].astype(bf16)

    def conv_back(grad_pre, c):
        ext_ref[0:T, c] = grad_pre
        raw = vs_ref[:, c].astype(f32)
        tap = taps_of(c, width, vtaps_ref, staps_ref)
        grad_raw = tap(0) * grad_pre
        csum_ref[8 * (K - 1) : 8 * K, c] += sum_rows(grad_pre * raw)
        csum_ref[8 * K : 8 * K + 8, c] += sum_rows(grad_pre)
        for s in range(1, K):
            moved = ext_ref[s : s + T, c] * keep[s - 1]
            grad_raw = grad_raw + tap(s) * moved
            csum_ref[8 * (K - 1 - s) : 8 * (K - s), c] += sum_rows(moved * raw)
        return grad_raw

    def slope(c):
        pre = pre_ref[:, c].astype(f32)
        logistic = sigmoid(pre)
        return logistic * (1.0 + pre * (1.0 - logistic))

    def through_of(value):
        high, low = two_terms(sum_rows(value))
        through = dot(high, er_ref[...]) + dot(low, er_ref[...])
        return jnp.broadcast_to(jnp.sum(through, axis=0, keepdims=True), (8, LANES))

    grad_scores = jnp.zeros((T, T), f32)
    through_ref[...] = through_of(sin_ref[0].astype(f32) * back_ref[...] * carry)
    for pair in range(width // LANES):
        c = slice(pair * LANES, (pair + 1) * LANES)
        x = act_ref[:, c].astype(f32)
        y = y_ref[:, c]
        g = mix_ref[:, c]
        grad_mix = g.astype(f32)
        step_x = ex_ref[0:T, c]
        dend_x = ex_ref[T : 2 * T, c]
        gd_ref[:, c] = (grad_mix * ex_ref[2 * T : 3 * T, c]).astype(bf16)
        xt_full = x * step_x
        xt = xt_full.astype(bf16)
        xd_ref[:, c] = (xt_full * dend_x).astype(bf16)
        zero = jnp.zeros_like(g)
        g_blocks = jnp.concatenate([jnp.where(first, g, zero), jnp.where(first, zero, g)], axis=0)
        x_blocks = jnp.concatenate([jnp.where(first, xt, zero), jnp.where(first, zero, xt)], axis=0)
        products = dot_nt(x_blocks, g)
        mixes = []
        for k, h in enumerate((2 * pair, 2 * pair + 1)):
            decay = jnp.exp(fade + (cum_t[h : h + 1, :] - cum[:, h : h + 1]))
            mixes.append((scores_t * decay).astype(bf16))
            grad_scores = grad_scores + products[k * T : (k + 1) * T] * decay
        u_in = dot(jnp.concatenate(mixes, axis=1), g_blocks)
        u_far = dend_x * dot(b_mat, back_bf[:, c])
        u = u_in + u_far
        y_far = ex_ref[2 * T : 3 * T, c] * dot(c_mat, sin_ref[0, :, c])
        xt_wide = xt.astype(f32)
        part_ref[0, :, c], part_ref[1, :, c] = two_terms(grad_mix * (y - y_far) - xt_wide * u_in)
        part_ref[2, :, c] = (grad_mix * y_far).astype(bf16)
        part_ref[3, :, c] = (xt_wide * u_far).astype(bf16)
        part_ref[4, :, c] = (x * u).astype(bf16)
        grad_value = step_x * u + skip_ref[pair : pair + 1, :] * grad_mix
        grad_ref[:, c] = conv_back(grad_value * slope(c), c).astype(bf16)

    gs_bf = grad_scores.astype(bf16)
    grad_b = dot(gs_bf, c_mat) + dot_nt(xd_ref[...], back_bf)
    grad_c = dot_tn(gs_bf, b_mat) + dot_nt(gd_ref[...], sin_ref[0])
    for k, grad in enumerate((grad_b, grad_c)):
        c = slice(width + k * N, width + (k + 1) * N)
        grad_ref[:, c] = conv_back(grad * slope(c), c).astype(bf16)
    ext_ref[T : T + 8, :] = ext_ref[0:8, :]

    by_head = [dot(part_ref[k], er_ref[...]) for k in range(5)]
    col_far, direct = by_head[3:]
    high, low = two_terms(by_head[0] + by_head[1] + by_head[2])
    grad_acc = through_ref[0:1, :] + (dot(triu_ref[...], high) + dot(triu_ref[...], low))
    high, low = two_terms(col_far)
    grad_acc = grad_acc + (dot(tri_ref[...], high) + dot(tri_ref[...], low)) - col_far
    grad_step = direct + grad_acc * rate
    grad_z = grad_step * sigmoid(z)
    csum_ref[8 * (K + 1) : 8 * (K + 2), 0:LANES] += sum_rows(grad_z)
    csum_ref[8 * (K + 1) : 8 * (K + 2), LANES : 2 * LANES] += sum_rows(grad_acc * step)
    grad_ref[:, width + 2 * N :] = grad_z.astype(bf16)

    new_back = back_ref[...] * carry + dot_tn(c_mat, gd_ref[...])
    back_ref[...] = new_back


def bits_of(size):
    return [1 << k for k in range(size.bit_length() - 1)] if size & (size - 1) == 0 else None


def swap(value, axis, size, bit):
    return lax.ppermute(value, axis, [(i, i ^ bit) for i in range(size)])


def block_of(rows):
    return max(b for b in range(16, 513, 16) if rows % b == 0)


def place(buffer, value, slot, dtype, mixed=False):
    rows, width = value.shape
    block = rows // 2 if mixed else block_of(rows)
    count = rows // block
    where = (lambda i, s: (2 * i + s[0], 0)) if mixed else (lambda i, s: (s[0] * count + i, 0))

    def kernel(slot_ref, value_ref, *refs):
        refs[-1][...] = value_ref[...].astype(dtype)

    out = jax.ShapeDtypeStruct((2 * rows, width), dtype)
    given = () if buffer is None else (buffer,)
    return pl.pallas_call(
        kernel,
        grid_spec=pltpu.PrefetchScalarGridSpec(
            num_scalar_prefetch=1,
            grid=(count,),
            in_specs=[pl.BlockSpec((block, width), lambda i, s: (i, 0))]
            + [pl.BlockSpec(memory_space=pl.ANY) for _ in given],
            out_specs=pl.BlockSpec((block, width), where),
        ),
        out_shape=out,
        input_output_aliases={2: 0} if given else {},
        name="place",
    )(jnp.reshape(slot, (1,)).astype(jnp.int32), value, *given)


def join(value, other, upper):
    rows, width = value.shape
    block = block_of(rows)
    count = rows // block

    def kernel(upper_ref, value_ref, other_ref, out_ref):
        mine = pl.program_id(0) == upper_ref[0]

        @pl.when(mine)
        def _():
            out_ref[...] = value_ref[...]

        @pl.when(jnp.logical_not(mine))
        def _():
            out_ref[...] = other_ref[...]

    return pl.pallas_call(
        kernel,
        grid_spec=pltpu.PrefetchScalarGridSpec(
            num_scalar_prefetch=1,
            grid=(2, count),
            in_specs=[
                pl.BlockSpec((block, width), lambda h, i, u: (jnp.where(h == u[0], i, 0), 0)),
                pl.BlockSpec((block, width), lambda h, i, u: (jnp.where(h == u[0], 0, i), 0)),
            ],
            out_specs=pl.BlockSpec((block, width), lambda h, i, u: (h * count + i, 0)),
        ),
        out_shape=jax.ShapeDtypeStruct((2 * rows, width), value.dtype),
        name="join",
    )(jnp.reshape(upper, (1,)).astype(jnp.int32), value, other)


def add_parts(parts, start, rows):
    total = None
    for value, base in parts:
        piece = lax.dynamic_slice_in_dim(value, base + start, rows, 0).astype(f32)
        total = piece if total is None else total + piece
    return total


def scatter_halves(kept, sent, axis, size):
    bits = bits_of(size)
    if size != 4:
        quarter = (2, kept.shape[0] // 2, kept.shape[1])
        value = jnp.stack([kept.reshape(quarter), sent.reshape(quarter)], axis=1)
        value = value.reshape(2 * kept.shape[0], kept.shape[1])
        return lax.psum_scatter(value, axis, scatter_dimension=0, tiled=True).astype(f32)
    other = swap(sent, axis, size, bits[0])
    return scatter_parts([(kept, 0), (other, 0)], axis, size, bits[1:])


def scatter_sum(value, axis, size):
    bits = bits_of(size)
    if bits is None:
        return lax.psum_scatter(value, axis, scatter_dimension=0, tiled=True).astype(f32)
    return scatter_parts([(value, 0)], axis, size, bits)


def scatter_parts(parts, axis, size, bits):
    index = lax.axis_index(axis)
    value = parts[0][0]
    rows = value.shape[0]
    for bit in bits:
        upper = (index // bit) % 2
        rows = rows // 2
        sent = add_parts(parts, (1 - upper) * rows, rows).astype(value.dtype)
        other = swap(sent, axis, size, bit)
        parts = [(part, base + upper * rows) for part, base in parts] + [(other, 0)]
    return add_parts(parts, 0, rows)


def gather_rows(value, axis, size, dtype, mixed=False):
    index = lax.axis_index(axis)
    bits = bits_of(size)
    if bits is None:
        return lax.all_gather(value, axis, axis=0, tiled=True).astype(dtype)
    for bit in bits[::-1]:
        other = swap(value, axis, size, bit)
        upper = (index // bit) % 2
        if bit == bits[0]:
            buffer = place(None, value, upper, dtype, mixed)
            value = place(buffer, other, 1 - upper, dtype, mixed)
        else:
            value = join(value, other, upper)
    return value.astype(dtype)


def reduce_rows(value, axis, size, dtype):
    part = scatter_sum(value, axis, size).astype(value.dtype)
    return gather_rows(part, axis, size, dtype)


def butterfly(value, axis, size):
    bits = bits_of(size)
    if bits is None:
        return lax.psum(value, axis)
    for bit in bits:
        value = value + swap(value, axis, size, bit)
    return value


def token_aux(segments):
    count = segments.shape[0]
    seg = segments.astype(f32)
    position = jnp.arange(count, dtype=jnp.int32) % SEQ_LEN
    columns = []
    lifted = []
    for s in range(1, K):
        before = jnp.concatenate([jnp.zeros((s,), f32), seg[:-s]])
        keep = ((position >= s) & (seg == before)).astype(f32)
        columns.append(keep)
        lifted.append(jnp.concatenate([keep[s:], jnp.zeros((s,), f32)]))
    chunked = seg.reshape(count // T, T)
    last = chunked[:, T - 1]
    starts = (jnp.arange(count // T, dtype=jnp.int32) * T) % SEQ_LEN == 0
    before = jnp.where(starts, -1.0, jnp.concatenate([jnp.zeros((1,), f32), last[:-1]]))
    columns.append((chunked == before[:, None]).astype(f32).reshape(count))
    columns.append((chunked == last[:, None]).astype(f32).reshape(count))
    columns.append(seg)
    rows = [row.reshape(count // T, T) for row in columns + lifted]
    return jnp.stack(rows + [rows[0]] * (16 - len(rows)), axis=1)


def group_kernel(
    _, gate_ref, packed_ref, normed_ref, gate_w, value_w, state_w, step_w,
    sent_ref, kept_ref, gain_ref, in_ref,
):
    weights = (value_w, state_w)
    steps = packed_ref[:, value_w.shape[1] + state_w.shape[1] :][:, : step_w.shape[0]]

    @pl.when(pl.program_id(0) == 0)
    def _():
        gain_ref[...] = jnp.zeros_like(gain_ref)

    model = in_ref.shape[1]
    part = model // 3 if model % 384 == 0 else model
    for lo in range(0, model, part):
        c = slice(lo, lo + part)
        total, at = dot_nt(gate_ref[...], gate_w[c, :]) + dot(steps, step_w[:, c]), 0
        for w in weights:
            total = total + dot_nt(packed_ref[:, at : at + w.shape[1]], w[c, :])
            at += w.shape[1]
        rounded = total.astype(bf16)
        in_ref[:, c] = rounded
        gain_ref[:, c] += sum_rows(rounded.astype(f32) * normed_ref[:, c].astype(f32))
    store_half(in_ref[...], sent_ref, kept_ref)


def on_device(
    tokens_in, segments, pre_gain, gate_proj, value_proj, state_proj, step_proj, conv_value,
    conv_value_bias, conv_state, conv_state_bias, step_bias, decay_log, skip_gain, norm_gain,
    out_proj, grad_out, *, n_dp, n_tensor,
):
    tokens, model = tokens_in.shape
    width = gate_proj.shape[1]
    heads = step_proj.shape[1]
    head_width = width // heads
    chunks = tokens // T
    seqs = tokens // SEQ_LEN
    per_seq = SEQ_LEN // T
    wide = width + 2 * N
    full = wide + LANES
    inner_width = width * n_tensor

    aux = token_aux(segments)

    projections = (gate_proj, value_proj, state_proj, step_proj.T)
    block = tokens // 4
    lead = 2 * T
    by_rows = lambda columns: pl.BlockSpec((lead, columns), lambda i: (i, 0))
    by_chunks = lambda *shape: pl.BlockSpec((lead // T,) + shape, lambda i: (i, 0, 0))
    held = lambda value: pl.BlockSpec(
        value.shape, lambda i: (0,) * value.ndim, pipeline_mode=pl.Buffered(1)
    )
    vbias = conv_value_bias.reshape(width // LANES, LANES)
    sbias = conv_state_bias.reshape(2 * N // LANES, LANES)
    head_pair = jnp.stack([step_bias, decay_log])
    decay_rate = -jnp.exp(decay_log)
    skip = jnp.repeat(skip_gain, head_width).reshape(width // LANES, LANES)
    gain = norm_gain.reshape(width // LANES, LANES)
    lanes = np.arange(LANES)
    owner = np.arange(width) // head_width
    expand = jnp.asarray(lanes[:, None] % HALF == owner[None, :], bf16)
    reduce = jnp.asarray(owner[:, None] == lanes[None, :], bf16)
    rows = np.arange(T)
    tri = jnp.asarray(rows[:, None] >= rows[None, :], bf16)
    triu = jnp.asarray(rows[:, None] <= rows[None, :], bf16)

    def at(block, index):
        return pl.BlockSpec(block, index)

    def whole(value):
        return pl.BlockSpec(value.shape, lambda i, j: (0,) * value.ndim, pipeline_mode=pl.Buffered(1))

    sds = jax.ShapeDtypeStruct
    pg_rows = pre_gain.reshape(model // LANES, LANES)
    consts = (pg_rows,) + projections + (out_proj, conv_value, conv_state, vbias, sbias)
    consts += (head_pair, skip, gain, expand, tri)
    normed, gate_raw, vs_raw, z_raw, grad_normed_out, y, act, pre, stat, sin = pl.pallas_call(
        lead_kernel,
        grid=(tokens // lead,),
        in_specs=[by_rows(model), by_rows(model), by_chunks(16, T)]
        + [held(v) for v in consts],
        out_specs=[by_rows(c) for c in (model, width, wide, LANES, width, width, wide, wide)]
        + [by_chunks(2, T), by_chunks(N, width)],
        out_shape=[
            sds((tokens, model), bf16), sds((tokens, width), bf16), sds((tokens, wide), bf16),
            sds((tokens, LANES), f32), sds((tokens, width), bf16), sds((tokens, width), f32),
            sds((tokens, wide), bf16), sds((tokens, wide), bf16), sds((chunks, 2, T), f32),
            sds((chunks, N, width), bf16),
        ],
        scratch_shapes=[
            pltpu.VMEM((lead + 8, wide), f32), pltpu.VMEM((N, width), f32),
            pltpu.VMEM((lead // T, 3 * T, width), f32), pltpu.VMEM((lead // T, 2, T, LANES), f32),
            pltpu.VMEM((8, LANES), f32),
        ],
        name="lead",
    )(tokens_in, grad_out, aux, *consts)

    if n_tensor == 4:
        others = [swap(stat, "tensor", n_tensor, bit) for bit in (1, 2, 3)]
        stat = (stat + others[0]) + (others[1] + others[2])
    else:
        stat = butterfly(stat, "tensor", n_tensor)
    scale = lax.rsqrt(stat[:, 0] / inner_width + eps_value)
    slope_scale = scale * scale * scale * stat[:, 1] / inner_width
    scales = jnp.stack([scale, slope_scale], axis=1)
    steps = tokens // block
    upper = lax.axis_index("tensor") % 2 if n_tensor == 4 else 0
    upper = jnp.reshape(jnp.asarray(upper, jnp.int32), (1,))
    turn = lambda i, u: jnp.where(i < 2, 2 * i + 1 - u[0], 2 * i - 4 + u[0])
    turned = lambda columns: pl.BlockSpec((block, columns), lambda i, u: (turn(i, u), 0))
    kept_spec = lambda columns: pl.BlockSpec(
        (block, columns), lambda i, u: (jnp.maximum(i - steps // 2, 0), 0)
    )
    sent_spec = lambda columns: pl.BlockSpec(
        (block, columns), lambda i, u: (jnp.minimum(i, steps // 2 - 1), 0)
    )
    fixed = lambda rows, columns: pl.BlockSpec((rows, columns), lambda i, u: (0, 0))
    still = lambda value: pl.BlockSpec(
        value.shape, lambda i, u: (0,) * value.ndim, pipeline_mode=pl.Buffered(1)
    )
    halves = [sds((tokens // 2, model), bf16)] * 2
    gate_bf, mix, normed_out, sent, kept, gate_sums = pl.pallas_call(
        middle_kernel,
        grid_spec=pltpu.PrefetchScalarGridSpec(
            num_scalar_prefetch=1,
            grid=(steps,),
            in_specs=[turned(width)] * 4
            + [pl.BlockSpec((block // T, 2, T), lambda i, u: (turn(i, u), 0, 0))]
            + [still(skip), still(gain), still(out_proj)],
            out_specs=[turned(width)] * 3
            + [sent_spec(model), kept_spec(model), fixed(16, width)],
        ),
        out_shape=[sds((tokens, width), bf16)] * 3 + halves + [sds((16, width), f32)],
        name="middle",
    )(upper, gate_raw, grad_normed_out, y, act, scales, skip, gain, out_proj)
    grad_out_proj = dot_tn(normed_out, grad_out).astype(bf16)
    grad_gate_proj = dot_tn(normed, gate_bf).astype(bf16)
    grad_out_proj = lax.psum(grad_out_proj, "dp")
    grad_out_proj = grad_out_proj.astype(f32)
    grad_gate_proj = reduce_rows(grad_gate_proj, "dp", n_dp, f32)

    start = lax.axis_index("tensor") * (tokens // n_tensor)
    own = lambda v: lax.dynamic_slice_in_dim(v, start, tokens // n_tensor, 0)
    branch = scatter_halves(kept, sent, "tensor", n_tensor)
    own_hidden = own(tokens_in).astype(f32)
    block_out = (own_hidden + branch).astype(bf16)
    if n_tensor == 4:
        block_out = gather_rows(block_out, "tensor", n_tensor, bf16, mixed=True)
    else:
        block_out = lax.all_gather(block_out, "tensor", axis=0, tiled=True)

    consts = (conv_value, conv_state, head_pair, skip, expand, reduce, tri, triu)
    bwd = lambda i, j: (i * per_seq + per_seq - 1 - j, 0)
    bwd3 = lambda i, j: (i * per_seq + per_seq - 1 - j, 0, 0)
    packed, csum = pl.pallas_call(
        backward_kernel,
        grid=(seqs, per_seq),
        in_specs=[
            at((T, width), bwd), at((T, width), bwd), at((T, wide), bwd), at((T, wide), bwd),
            at((T, wide), bwd), at((T, LANES), bwd), at((1, N, width), bwd3),
            at((1, 16, T), bwd3),
        ] + [whole(v) for v in consts],
        out_specs=[
            at((T, full), bwd), pl.BlockSpec((8 * (K + 2), wide), lambda i, j: (0, 0)),
        ],
        out_shape=[sds((tokens, full), bf16), sds((8 * (K + 2), wide), f32)],
        scratch_shapes=[
            pltpu.VMEM((N, width), f32), pltpu.VMEM((T + 8, wide), f32),
            pltpu.VMEM((3 * T, width), f32), pltpu.VMEM((T, width), bf16),
            pltpu.VMEM((T, width), bf16), pltpu.VMEM((8, LANES), f32),
            pltpu.VMEM((8, LANES), f32), pltpu.VMEM((5, T, width), bf16),
        ],
        name="ssd_backward",
    )(mix, y, act, pre, vs_raw, z_raw, sin, aux, *consts)

    grad_value_proj = dot_tn(normed, packed[:, :width]).astype(bf16)
    grad_state_proj = dot_tn(normed, packed[:, width:wide]).astype(bf16)
    grad_step_proj = dot_tn(packed[:, wide:], normed)[:heads]
    sent, kept, gain_part = pl.pallas_call(
        group_kernel,
        grid_spec=pltpu.PrefetchScalarGridSpec(
            num_scalar_prefetch=1,
            grid=(steps,),
            in_specs=[turned(width), turned(full), turned(model)]
            + [still(w) for w in projections],
            out_specs=[sent_spec(model), kept_spec(model), fixed(8, model)],
            scratch_shapes=[pltpu.VMEM((block, model), bf16)],
        ),
        out_shape=halves + [sds((8, model), f32)],
        name="group_in",
    )(upper, gate_bf, packed, normed, *projections)
    gate_sums = jnp.pad(gate_sums, ((0, 0), (0, 2 * N)))
    sums = jnp.sum(jnp.concatenate([csum, gate_sums]).reshape(K + 4, 8, wide), axis=1)
    gain_part = jnp.sum(gain_part, axis=0) / pre_gain

    grad_value_proj = reduce_rows(grad_value_proj, "dp", n_dp, f32)

    grad_normed = scatter_halves(kept, sent, "tensor", n_tensor)
    tokens_late, _ = lax.optimization_barrier((tokens_in, kept))
    own_hidden = own(tokens_late).astype(f32)
    own_inv = lax.rsqrt(jnp.mean(own_hidden * own_hidden, axis=1, keepdims=True) + eps_value)
    weighted = pre_gain * grad_normed
    grad_hidden = own_inv * weighted - own_hidden * (own_inv * own_inv * own_inv) * jnp.mean(
        weighted * own_hidden, axis=1, keepdims=True
    )
    grad_in = (own(grad_out).astype(f32) + grad_hidden).astype(bf16)
    grad_in = lax.all_gather(grad_in, "tensor", axis=0, tiled=True)

    gain_rows = model // (2 * N)
    extra = jnp.concatenate([sums[:, width:], gain_part.reshape(gain_rows, 2 * N)], axis=0)
    unit = n_tensor * math.lcm(16, model // math.gcd(model, 2 * N))
    gap = -(model + extra.shape[0]) % unit
    extra = jnp.pad(extra, ((0, gap), (0, 0))).astype(bf16)
    shared = jnp.concatenate([grad_state_proj, extra], axis=0)
    shared = scatter_sum(shared, "tensor", n_tensor).astype(bf16)
    small = jnp.concatenate([jnp.pad(sums, ((0, 0), (0, model - wide))), grad_step_proj], axis=0)
    part = shared.shape[0]
    flat = part * 2 * N // model
    both = jnp.concatenate([shared.reshape(flat, model), small.astype(bf16)], axis=0)
    both = butterfly(both, "dp", n_dp)
    shared, small = both[:flat].reshape(part, 2 * N), both[flat:].astype(f32)
    shared = gather_rows(shared, "tensor", n_tensor, bf16)
    grad_state_proj = shared[:model].astype(f32)
    state_sums = shared[model : model + K + 4].astype(f32)
    grad_pre_gain = shared[model + K + 4 : model + K + 4 + gain_rows].reshape(model).astype(f32)
    sums = small[: K + 4]
    grad_step_proj = small[K + 4 :].T
    grad_skip = jnp.sum(sums[K + 3, :width].reshape(heads, head_width), axis=1)
    return (
        block_out,
        grad_in,
        grad_pre_gain,
        grad_gate_proj,
        grad_value_proj,
        grad_state_proj,
        grad_step_proj,
        sums[:K, :width],
        sums[K, :width],
        state_sums[:K],
        state_sums[K],
        sums[K + 1, :heads],
        sums[K + 1, LANES : LANES + heads] * decay_rate,
        grad_skip,
        sums[K + 2, :width],
        grad_out_proj,
    )


def solution(mesh):
    t = P("tensor")
    cols = P(None, "tensor")
    in_specs = (
        P("dp", None), P("dp"), P(), cols, cols, P(), cols, cols, t, P(), P(), t, t, t, t,
        P("tensor", None), P("dp", None),
    )
    out_specs = (
        P("dp", None), P("dp", None), P(), cols, cols, P(), cols, cols, t, P(), P(), t, t, t, t,
        P("tensor", None),
    )
    n_dp, n_tensor = mesh.shape["dp"], mesh.shape["tensor"]

    def body(*args):
        return on_device(*args, n_dp=n_dp, n_tensor=n_tensor)

    return jax.shard_map(body, mesh=mesh, in_specs=in_specs, out_specs=out_specs, check_vma=False)
```

```python
import math

import jax
import jax.numpy as jnp
from jax import lax
from jax.experimental import pallas as pl
from jax.experimental.pallas import tpu as pltpu
from jax.sharding import PartitionSpec as P


N = 128
K = 4
SEQ_LEN = 1024
T = 128
LANES = 128
HALF = 64
NEG = -1e30
eps_value = 1e-05
f32 = jnp.float32
bf16 = jnp.bfloat16


def dot(a, b):
    return jnp.dot(a, b, preferred_element_type=f32)


def dot_nt(a, b):
    return lax.dot_general(a, b, (((1,), (1,)), ((), ())), preferred_element_type=f32)


def dot_tn(a, b):
    return lax.dot_general(a, b, (((0,), (0,)), ((), ())), preferred_element_type=f32)


def sigmoid(v):
    return 0.5 * jnp.tanh(0.5 * v) + 0.5


def two_terms(v):
    high = v.astype(bf16)
    return high, (v - high.astype(f32)).astype(bf16)


def paired(v):
    high, low = two_terms(v)
    lane = lax.broadcasted_iota(jnp.int32, v.shape, 1)
    return jnp.where(lane < HALF, high, low)


def sum_rows(v):
    total = v[0:8]
    for row in range(8, v.shape[0], 8):
        total = total + v[row : row + 8]
    return total


def head_rows(heads_ref, lane_ref):
    count = heads_ref.shape[1]
    lane_ref[...] = jnp.zeros_like(lane_ref)
    lane_ref[0:2, 0:count] = heads_ref[...]
    lane_ref[0:2, HALF : HALF + count] = heads_ref[...]
    return lane_ref[0:1, :], -jnp.exp(lane_ref[1:2, :])


def ones_where(condition):
    return jnp.where(condition, 1.0, 0.0).astype(bf16)


def expansion(shape, head_width):
    lane = lax.broadcasted_iota(jnp.int32, shape, 0)
    owner = lax.broadcasted_iota(jnp.int32, shape, 1) // head_width
    return ones_where((lane == owner) | (lane == owner + HALF))


def reduction(shape, head_width):
    owner = lax.broadcasted_iota(jnp.int32, shape, 0) // head_width
    return ones_where(lax.broadcasted_iota(jnp.int32, shape, 1) == owner)


def triangle():
    row = lax.broadcasted_iota(jnp.int32, (T, T), 0)
    col = lax.broadcasted_iota(jnp.int32, (T, T), 1)
    return row, col


def head_terms(z_ref, bias, rate, aux, tri, e_ref, ex_ref):
    z = z_ref[...] + bias
    tail = jnp.exp(-jnp.abs(z))
    step = jnp.maximum(z, 0.0) + jnp.log1p(tail)
    high, low = two_terms(step * rate)
    cum = dot(tri, high) + dot(tri, low)
    end = cum[T - 1 : T]
    dst = jnp.exp(cum) * aux[:, 3:4]
    dend = jnp.exp(end - cum) * aux[:, 4:5]
    total = jnp.exp(jnp.broadcast_to(end, (8, LANES))) * aux[T - 1 : T, 3:4]
    stacked = jnp.concatenate([paired(step), paired(dend), paired(dst)], axis=0)
    ex_ref[...] = dot(stacked, e_ref[...])
    carry = dot(paired(total), e_ref[...])[0:1]
    return z, step, cum, cum.T, carry


def taps_of(c, width, vtaps_ref, staps_ref):
    ref, at = (vtaps_ref, c) if c.start < width else (staps_ref, slice(c.start - width, c.stop - width))
    return lambda s: ref[K - 1 - s : K - s, at]


def lead_kernel(
    tokens_ref, go_ref, aux_ref, pg_ref, gate_w, value_w, state_w, step_w, out_w,
    vtaps_ref, staps_ref, vbias_ref, sbias_ref, heads_ref, skip_ref, ng_ref,
    normed_ref, gate_ref, vs_ref, z_ref, gno_ref, y_ref, act_ref, pre_ref, stat_ref, sin_ref,
    ext_ref, state_ref, ex_ref, sum_ref, lane_ref, e_ref,
):
    rows, width = gate_ref.shape
    chunks = range(rows // T)

    @pl.when(pl.program_id(0) == 0)
    def _():
        e_ref[...] = expansion(e_ref.shape, width // heads_ref.shape[1])

    @pl.when(pl.program_id(0) % (SEQ_LEN // rows) == 0)
    def _():
        state_ref[...] = jnp.zeros_like(state_ref)
        ext_ref[0:8, :] = jnp.zeros_like(ext_ref[0:8, :])

    part = 32

    def normalize(index, carry):
        r = pl.ds(pl.multiple_of(index * part, part), part)
        hidden = tokens_ref[r, :].astype(f32)
        inv = lax.rsqrt(jnp.mean(hidden * hidden, axis=1, keepdims=True) + eps_value)
        for k in range(pg_ref.shape[0]):
            c = slice(k * LANES, (k + 1) * LANES)
            normed_ref[r, c] = (hidden[:, c] * inv * pg_ref[k : k + 1, :]).astype(bf16)
        return carry

    lax.fori_loop(0, rows // part, normalize, 0)
    z = dot_nt(normed_ref[...], step_w[...])
    z_ref[...] = jnp.zeros_like(z_ref)
    z_ref[:, : z.shape[1]] = z
    z_ref[:, HALF : HALF + z.shape[1]] = z
    raw = dot(normed_ref[...], state_w[...])
    ext_ref[8:, width:] = raw
    vs_ref[:, width:] = raw.astype(bf16)
    at = [pl.ds(k * T, T) for k in chunks]
    bias, rate = head_rows(heads_ref, lane_ref)
    row, col = triangle()
    tri = ones_where(row >= col)
    aux = [aux_ref[k].T for k in chunks]
    terms = [
        head_terms(z_ref.at[at[k]], bias, rate, aux[k], tri, e_ref, ex_ref.at[k])
        for k in chunks
    ]
    keep = [
        [jnp.broadcast_to(aux[k][:, s : s + 1], (T, LANES)) for s in range(K - 1)] for k in chunks
    ]

    def activate(c, k):
        lo = 8 + k * T
        tap, shift = taps_of(c, width, vtaps_ref, staps_ref), c.start // LANES
        if c.start < width:
            pre = vbias_ref[shift : shift + 1, :]
        else:
            pre = sbias_ref[shift - width // LANES : shift - width // LANES + 1, :]
        pre = pre + tap(0) * ext_ref[lo : lo + T, c]
        for s in range(1, K):
            pre = pre + tap(s) * (ext_ref[lo - s : lo - s + T, c] * keep[k][s - 1])
        half = 0.5 * pre
        act = half + half * jnp.tanh(half)
        act_bf = act.astype(bf16)
        pre_ref[at[k], c] = pre.astype(bf16)
        act_ref[at[k], c] = act_bf
        return act, act_bf

    b_flip, c_mats, scores, fades = [], [], [], []
    for k in chunks:
        _, b_mat = activate(slice(width, width + N), k)
        _, c_mat = activate(slice(width + N, width + 2 * N), k)
        b_flip.append(b_mat.T)
        c_mats.append(c_mat)
        scores.append(dot_nt(c_mat, b_mat))
        same = (aux[k][:, 5:6] == aux_ref[k, 5:6, :]) & (row >= col)
        fades.append(jnp.where(same, 0.0, NEG))
    first = lax.broadcasted_iota(jnp.int32, (T, LANES), 1) < HALF
    sum_ref[...] = jnp.zeros_like(sum_ref)
    span = 2 * LANES if width % (2 * LANES) == 0 else LANES
    for lo in range(0, width, span):
        group = slice(lo, lo + span)
        raw = dot(normed_ref[...], value_w[:, group])
        ext_ref[8:, group] = raw
        vs_ref[:, group] = raw.astype(bf16)
        gates = dot(normed_ref[...], gate_w[:, group])
        gate_ref[:, group] = gates.astype(bf16)
        gnos = dot_nt(go_ref[...], out_w[group, :])
        gno_ref[:, group] = gnos.astype(bf16)
        for pair in range(lo // LANES, (lo + span) // LANES):
            c = slice(pair * LANES, (pair + 1) * LANES)
            inside = slice(pair * LANES - lo, (pair + 1) * LANES - lo)
            for k in chunks:
                _, _, cum, cum_t, carry = terms[k]
                r = slice(k * T, (k + 1) * T)
                act, act_bf = activate(c, k)
                xt_full = act_bf.astype(f32) * ex_ref[k, 0:T, c]
                xt = xt_full.astype(bf16)
                xd = (xt_full * ex_ref[k, T : 2 * T, c]).astype(bf16)
                mixes = []
                for h in (2 * pair, 2 * pair + 1):
                    decay = jnp.exp(fades[k] + (cum[:, h : h + 1] - cum_t[h : h + 1, :]))
                    mixes.append((scores[k] * decay).astype(bf16))
                zero = jnp.zeros_like(xt)
                blocks = [jnp.where(first, xt, zero), jnp.where(first, zero, xt)]
                state = state_ref[:, c]
                state_bf = state.astype(bf16)
                sin_ref[k, :, c] = state_bf
                y = dot(jnp.concatenate(mixes, axis=1), jnp.concatenate(blocks, axis=0))
                y = y + ex_ref[k, 2 * T : 3 * T, c] * dot(c_mats[k], state_bf)
                y_ref[r, c] = y
                state_ref[:, c] = state * carry[:, c] + dot(b_flip[k], xd)
                half = 0.5 * gates[r, inside]
                gated = (y + skip_ref[pair : pair + 1, :] * act) * (half + half * jnp.tanh(half))
                sum_ref[k, 0] += gated * gated
                sum_ref[k, 1] += gated * ng_ref[pair : pair + 1, :] * gnos[r, inside]
    for k in chunks:
        for s in range(2):
            stat_ref[k, s : s + 1, :] = jnp.sum(sum_ref[k, s].T, axis=0, keepdims=True)
    ext_ref[0:8, :] = ext_ref[rows : rows + 8, :]


def store_half(value, sent_ref, kept_ref):
    first = pl.program_id(0) < pl.num_programs(0) // 2

    @pl.when(first)
    def _():
        sent_ref[...] = value

    @pl.when(jnp.logical_not(first))
    def _():
        kept_ref[...] = value


def middle_kernel(
    _, gate_ref, gno_ref, y_ref, act_ref, stat_ref, skip_ref, ng_ref, out_w,
    gate_grad_ref, mix_ref, normed_ref, sent_ref, kept_ref, csum_ref,
):
    @pl.when(pl.program_id(0) == 0)
    def _():
        csum_ref[...] = jnp.zeros_like(csum_ref)

    def one(chunk, carry):
        r = pl.ds(pl.multiple_of(chunk * T, T), T)
        scale = jnp.broadcast_to(stat_ref[chunk, 0:1, :], (LANES, T)).T
        slope_scale = jnp.broadcast_to(stat_ref[chunk, 1:2, :], (LANES, T)).T
        for pair in range(gate_ref.shape[1] // LANES):
            c = slice(pair * LANES, (pair + 1) * LANES)
            gate = gate_ref[r, c].astype(f32)
            logistic = sigmoid(gate)
            swish = gate * logistic
            x = act_ref[r, c].astype(f32)
            gno = gno_ref[r, c].astype(f32)
            ssd = y_ref[r, c] + skip_ref[pair : pair + 1, :] * x
            gated = ssd * swish
            unit = gated * scale
            normed_ref[r, c] = (unit * ng_ref[pair : pair + 1, :]).astype(bf16)
            grad_gated = scale * (gno * ng_ref[pair : pair + 1, :]) - slope_scale * gated
            csum_ref[0:8, c] += sum_rows(gno * unit)
            grad_mix = grad_gated * swish
            grad_gate = grad_gated * ssd * (logistic + swish * (1.0 - logistic))
            gate_grad_ref[r, c] = grad_gate.astype(bf16)
            csum_ref[8:16, c] += sum_rows(grad_mix * x)
            mix_ref[r, c] = grad_mix.astype(bf16)
        return carry

    lax.fori_loop(0, stat_ref.shape[0], one, 0)
    store_half(dot(normed_ref[...], out_w[...]).astype(bf16), sent_ref, kept_ref)


def backward_kernel(
    mix_ref, y_ref, act_ref, pre_ref, vs_ref, z_ref, sin_ref, aux_ref,
    vtaps_ref, staps_ref, heads_ref, skip_ref,
    grad_ref, csum_ref,
    back_ref, ext_ref, ex_ref, xd_ref, gd_ref, through_ref, lane_ref, part_ref, e_ref, er_ref,
):
    width = mix_ref.shape[1]

    @pl.when((pl.program_id(0) == 0) & (pl.program_id(1) == 0))
    def _():
        csum_ref[...] = jnp.zeros_like(csum_ref)
        e_ref[...] = expansion(e_ref.shape, width // heads_ref.shape[1])
        er_ref[...] = reduction(er_ref.shape, width // heads_ref.shape[1])

    @pl.when(pl.program_id(1) == 0)
    def _():
        back_ref[...] = jnp.zeros_like(back_ref)
        ext_ref[T : T + 8, :] = jnp.zeros_like(ext_ref[T : T + 8, :])

    row, col = triangle()
    tri, triu = ones_where(row >= col), ones_where(row <= col)
    bias, rate = head_rows(heads_ref, lane_ref)
    aux = aux_ref[0].T
    z, step, cum, cum_t, carry = head_terms(z_ref, bias, rate, aux, tri, e_ref, ex_ref)
    keep = [jnp.broadcast_to(aux[:, 5 + s : 6 + s], (T, LANES)) for s in range(1, K)]
    b_mat = act_ref[:, width : width + N]
    c_mat = act_ref[:, width + N : width + 2 * N]
    scores_t = dot_nt(b_mat, c_mat)
    same = (aux[:, 5:6] == aux_ref[0, 5:6, :]) & (row <= col)
    fade = jnp.where(same, 0.0, NEG)
    lane = lax.broadcasted_iota(jnp.int32, (T, LANES), 1)
    first = lane < HALF
    back_bf = back_ref[...].astype(bf16)

    def conv_back(grad_pre, c):
        ext_ref[0:T, c] = grad_pre
        raw = vs_ref[:, c].astype(f32)
        tap = taps_of(c, width, vtaps_ref, staps_ref)
        grad_raw = tap(0) * grad_pre
        csum_ref[8 * (K - 1) : 8 * K, c] += sum_rows(grad_pre * raw)
        csum_ref[8 * K : 8 * K + 8, c] += sum_rows(grad_pre)
        for s in range(1, K):
            moved = ext_ref[s : s + T, c] * keep[s - 1]
            grad_raw = grad_raw + tap(s) * moved
            csum_ref[8 * (K - 1 - s) : 8 * (K - s), c] += sum_rows(moved * raw)
        return grad_raw

    def slope(c):
        pre = pre_ref[:, c].astype(f32)
        logistic = sigmoid(pre)
        return logistic * (1.0 + pre * (1.0 - logistic))

    def through_of(value):
        high, low = two_terms(sum_rows(value))
        through = dot(high, er_ref[...]) + dot(low, er_ref[...])
        return jnp.broadcast_to(jnp.sum(through, axis=0, keepdims=True), (8, LANES))

    grad_scores = jnp.zeros((T, T), f32)
    through_ref[...] = through_of(sin_ref[0].astype(f32) * back_ref[...] * carry)
    for pair in range(width // LANES):
        c = slice(pair * LANES, (pair + 1) * LANES)
        x = act_ref[:, c].astype(f32)
        y = y_ref[:, c]
        g = mix_ref[:, c]
        grad_mix = g.astype(f32)
        step_x = ex_ref[0:T, c]
        dend_x = ex_ref[T : 2 * T, c]
        gd_ref[:, c] = (grad_mix * ex_ref[2 * T : 3 * T, c]).astype(bf16)
        xt_full = x * step_x
        xt = xt_full.astype(bf16)
        xd_ref[:, c] = (xt_full * dend_x).astype(bf16)
        zero = jnp.zeros_like(g)
        g_blocks = jnp.concatenate([jnp.where(first, g, zero), jnp.where(first, zero, g)], axis=0)
        x_blocks = jnp.concatenate([jnp.where(first, xt, zero), jnp.where(first, zero, xt)], axis=0)
        products = dot_nt(x_blocks, g)
        mixes = []
        for k, h in enumerate((2 * pair, 2 * pair + 1)):
            decay = jnp.exp(fade + (cum_t[h : h + 1, :] - cum[:, h : h + 1]))
            mixes.append((scores_t * decay).astype(bf16))
            grad_scores = grad_scores + products[k * T : (k + 1) * T] * decay
        u_in = dot(jnp.concatenate(mixes, axis=1), g_blocks)
        u_far = dend_x * dot(b_mat, back_bf[:, c])
        u = u_in + u_far
        y_far = ex_ref[2 * T : 3 * T, c] * dot(c_mat, sin_ref[0, :, c])
        xt_wide = xt.astype(f32)
        part_ref[0, :, c], part_ref[1, :, c] = two_terms(grad_mix * (y - y_far) - xt_wide * u_in)
        part_ref[2, :, c] = (grad_mix * y_far).astype(bf16)
        part_ref[3, :, c] = (xt_wide * u_far).astype(bf16)
        part_ref[4, :, c] = (x * u).astype(bf16)
        grad_value = step_x * u + skip_ref[pair : pair + 1, :] * grad_mix
        grad_ref[:, c] = conv_back(grad_value * slope(c), c).astype(bf16)

    gs_bf = grad_scores.astype(bf16)
    grad_b = dot(gs_bf, c_mat) + dot_nt(xd_ref[...], back_bf)
    grad_c = dot_tn(gs_bf, b_mat) + dot_nt(gd_ref[...], sin_ref[0])
    for k, grad in enumerate((grad_b, grad_c)):
        c = slice(width + k * N, width + (k + 1) * N)
        grad_ref[:, c] = conv_back(grad * slope(c), c).astype(bf16)
    ext_ref[T : T + 8, :] = ext_ref[0:8, :]

    by_head = [dot(part_ref[k], er_ref[...]) for k in range(5)]
    col_far, direct = by_head[3:]
    high, low = two_terms(by_head[0] + by_head[1] + by_head[2])
    grad_acc = through_ref[0:1, :] + (dot(triu, high) + dot(triu, low))
    high, low = two_terms(col_far)
    grad_acc = grad_acc + (dot(tri, high) + dot(tri, low)) - col_far
    grad_step = direct + grad_acc * rate
    grad_z = grad_step * sigmoid(z)
    csum_ref[8 * (K + 1) : 8 * (K + 2), 0:LANES] += sum_rows(grad_z)
    csum_ref[8 * (K + 1) : 8 * (K + 2), LANES : 2 * LANES] += sum_rows(grad_acc * step)
    grad_ref[:, width + 2 * N :] = grad_z.astype(bf16)

    new_back = back_ref[...] * carry + dot_tn(c_mat, gd_ref[...])
    back_ref[...] = new_back


def bits_of(size):
    return [1 << k for k in range(size.bit_length() - 1)] if size & (size - 1) == 0 else None


def swap(value, axis, size, bit):
    return lax.ppermute(value, axis, [(i, i ^ bit) for i in range(size)])


def block_of(rows):
    return max(b for b in range(16, 513, 16) if rows % b == 0)


def place(buffer, value, slot, dtype, mixed=False):
    rows, width = value.shape
    block = rows // 2 if mixed else block_of(rows)
    count = rows // block
    where = (lambda i, s: (2 * i + s[0], 0)) if mixed else (lambda i, s: (s[0] * count + i, 0))

    def kernel(slot_ref, value_ref, *refs):
        refs[-1][...] = value_ref[...].astype(dtype)

    out = jax.ShapeDtypeStruct((2 * rows, width), dtype)
    given = () if buffer is None else (buffer,)
    return pl.pallas_call(
        kernel,
        grid_spec=pltpu.PrefetchScalarGridSpec(
            num_scalar_prefetch=1,
            grid=(count,),
            in_specs=[pl.BlockSpec((block, width), lambda i, s: (i, 0))]
            + [pl.BlockSpec(memory_space=pl.ANY) for _ in given],
            out_specs=pl.BlockSpec((block, width), where),
        ),
        out_shape=out,
        input_output_aliases={2: 0} if given else {},
        name="place",
    )(jnp.reshape(slot, (1,)).astype(jnp.int32), value, *given)


def copy_rows(value):
    def kernel(value_ref, out_ref):
        out_ref[...] = value_ref[...]

    spec = pl.BlockSpec((block_of(value.shape[0]), value.shape[1]), lambda i: (i, 0))
    return pl.pallas_call(
        kernel,
        grid=(value.shape[0] // spec.block_shape[0],),
        in_specs=[spec],
        out_specs=spec,
        out_shape=jax.ShapeDtypeStruct(value.shape, value.dtype),
        name="copy_rows",
    )(value)


def join(value, other, upper):
    rows, width = value.shape
    block = block_of(rows)
    count = rows // block

    def kernel(upper_ref, value_ref, other_ref, out_ref):
        mine = pl.program_id(0) == upper_ref[0]

        @pl.when(mine)
        def _():
            out_ref[...] = value_ref[...]

        @pl.when(jnp.logical_not(mine))
        def _():
            out_ref[...] = other_ref[...]

    return pl.pallas_call(
        kernel,
        grid_spec=pltpu.PrefetchScalarGridSpec(
            num_scalar_prefetch=1,
            grid=(2, count),
            in_specs=[
                pl.BlockSpec((block, width), lambda h, i, u: (jnp.where(h == u[0], i, 0), 0)),
                pl.BlockSpec((block, width), lambda h, i, u: (jnp.where(h == u[0], 0, i), 0)),
            ],
            out_specs=pl.BlockSpec((block, width), lambda h, i, u: (h * count + i, 0)),
        ),
        out_shape=jax.ShapeDtypeStruct((2 * rows, width), value.dtype),
        name="join",
    )(jnp.reshape(upper, (1,)).astype(jnp.int32), value, other)


def add_parts(parts, start, rows):
    total = None
    for value, base in parts:
        piece = lax.dynamic_slice_in_dim(value, base + start, rows, 0).astype(f32)
        total = piece if total is None else total + piece
    return total


def sum_quarters(kept, sent, arrays, rows, kernel):
    index = lax.axis_index("tensor")
    other = swap(sent, "tensor", 4, 1)
    upper = index // 2
    quarter, width = kept.shape[0] // 2, kept.shape[1]
    out = add_parts([(kept, 0), (other, 0)], (1 - upper) * quarter, quarter).astype(kept.dtype)
    last = swap(out, "tensor", 4, 2)
    count = quarter // T
    half = pl.BlockSpec((T, width), lambda i, s: (s[1] * count + i, 0))
    own = pl.BlockSpec((T, width), lambda i, s: (s[0] * count + i, 0))
    plain = pl.BlockSpec((T, width), lambda i, s: (i, 0))
    return pl.pallas_call(
        kernel,
        grid_spec=pltpu.PrefetchScalarGridSpec(
            num_scalar_prefetch=1,
            grid=(count,),
            in_specs=[half, half, plain]
            + [own for _ in arrays]
            + [pl.BlockSpec(v.shape, lambda i, s: (0, 0)) for v in rows],
            out_specs=plain,
        ),
        out_shape=jax.ShapeDtypeStruct((quarter, width), bf16),
        name="quarter",
    )(jnp.stack([index, upper]).astype(jnp.int32), kept, other, last, *arrays, *rows)


def block_kernel(_, kept_ref, other_ref, last_ref, tokens_ref, out_ref):
    total = kept_ref[...].astype(f32) + other_ref[...].astype(f32) + last_ref[...].astype(f32)
    out_ref[...] = (tokens_ref[...].astype(f32) + total).astype(bf16)


def input_kernel(_, kept_ref, other_ref, last_ref, tokens_ref, grad_ref, gain_ref, out_ref):
    part = 32

    def one(index, carry):
        r = pl.ds(pl.multiple_of(index * part, part), part)
        total = kept_ref[r, :].astype(f32) + other_ref[r, :].astype(f32) + last_ref[r, :].astype(f32)
        hidden = tokens_ref[r, :].astype(f32)
        inv = lax.rsqrt(jnp.mean(hidden * hidden, axis=1, keepdims=True) + eps_value)
        weighted = gain_ref[0:1, :] * total
        mean = jnp.mean(weighted * hidden, axis=1, keepdims=True)
        grad_hidden = inv * weighted - hidden * (inv * inv * inv * mean)
        out_ref[r, :] = (grad_ref[r, :].astype(f32) + grad_hidden).astype(bf16)
        return carry

    lax.fori_loop(0, out_ref.shape[0] // part, one, 0)


def scatter_halves(kept, sent, axis, size):
    bits = bits_of(size)
    if size != 4:
        quarter = (2, kept.shape[0] // 2, kept.shape[1])
        value = jnp.stack([kept.reshape(quarter), sent.reshape(quarter)], axis=1)
        value = value.reshape(2 * kept.shape[0], kept.shape[1])
        return lax.psum_scatter(value, axis, scatter_dimension=0, tiled=True).astype(f32)
    other = swap(sent, axis, size, bits[0])
    return scatter_parts([(kept, 0), (other, 0)], axis, size, bits[1:])


def scatter_sum(value, axis, size):
    bits = bits_of(size)
    if bits is None:
        return lax.psum_scatter(value, axis, scatter_dimension=0, tiled=True).astype(f32)
    return scatter_parts([(value, 0)], axis, size, bits)


def scatter_parts(parts, axis, size, bits):
    index = lax.axis_index(axis)
    value = parts[0][0]
    rows = value.shape[0]
    for bit in bits:
        upper = (index // bit) % 2
        rows = rows // 2
        sent = add_parts(parts, (1 - upper) * rows, rows).astype(value.dtype)
        other = swap(sent, axis, size, bit)
        parts = [(part, base + upper * rows) for part, base in parts] + [(other, 0)]
    return add_parts(parts, 0, rows)


def gather_rows(value, axis, size, dtype, mixed=False):
    index = lax.axis_index(axis)
    bits = bits_of(size)
    if bits is None:
        return lax.all_gather(value, axis, axis=0, tiled=True).astype(dtype)
    for bit in bits[::-1]:
        other = swap(value, axis, size, bit)
        upper = (index // bit) % 2
        if bit == bits[0]:
            buffer = place(None, value, upper, dtype, mixed)
            value = place(buffer, other, 1 - upper, dtype, mixed)
        else:
            value = join(value, other, upper)
    return value.astype(dtype)


def reduce_rows(value, axis, size, dtype):
    part = scatter_sum(value, axis, size).astype(value.dtype)
    return gather_rows(part, axis, size, dtype)


def butterfly(value, axis, size):
    bits = bits_of(size)
    if bits is None:
        return lax.psum(value, axis)
    for bit in bits:
        value = value + swap(value, axis, size, bit)
    return value


def token_aux(segments):
    count = segments.shape[0]
    seg = segments.astype(f32)
    position = jnp.arange(count, dtype=jnp.int32) % SEQ_LEN
    columns = []
    lifted = []
    for s in range(1, K):
        before = jnp.concatenate([jnp.zeros((s,), f32), seg[:-s]])
        keep = ((position >= s) & (seg == before)).astype(f32)
        columns.append(keep)
        lifted.append(jnp.concatenate([keep[s:], jnp.zeros((s,), f32)]))
    chunked = seg.reshape(count // T, T)
    last = chunked[:, T - 1]
    starts = (jnp.arange(count // T, dtype=jnp.int32) * T) % SEQ_LEN == 0
    before = jnp.where(starts, -1.0, jnp.concatenate([jnp.zeros((1,), f32), last[:-1]]))
    columns.append((chunked == before[:, None]).astype(f32).reshape(count))
    columns.append((chunked == last[:, None]).astype(f32).reshape(count))
    columns.append(seg)
    rows = [row.reshape(count // T, T) for row in columns + lifted]
    return jnp.stack(rows + [rows[0]] * (16 - len(rows)), axis=1)


def group_kernel(
    _, gate_ref, packed_ref, normed_ref, gate_w, value_w, state_w, step_w,
    sent_ref, kept_ref, gain_ref, in_ref,
):
    weights = (value_w, state_w)
    steps = packed_ref[:, value_w.shape[1] + state_w.shape[1] :][:, : step_w.shape[0]]

    @pl.when(pl.program_id(0) == 0)
    def _():
        gain_ref[...] = jnp.zeros_like(gain_ref)

    model = in_ref.shape[1]
    part = model // 3 if model % 384 == 0 else model

    def one(index, carry):
        c = pl.ds(pl.multiple_of(index * part, part), part)
        total, at = dot_nt(gate_ref[...], gate_w[c, :]) + dot(steps, step_w[:, c]), 0
        for w in weights:
            total = total + dot_nt(packed_ref[:, at : at + w.shape[1]], w[c, :])
            at += w.shape[1]
        rounded = total.astype(bf16)
        in_ref[:, c] = rounded
        gain_ref[:, c] += sum_rows(rounded.astype(f32) * normed_ref[:, c].astype(f32))
        return carry

    lax.fori_loop(0, model // part, one, 0)
    store_half(in_ref[...], sent_ref, kept_ref)


def on_device(
    tokens_in, segments, pre_gain, gate_proj, value_proj, state_proj, step_proj, conv_value,
    conv_value_bias, conv_state, conv_state_bias, step_bias, decay_log, skip_gain, norm_gain,
    out_proj, grad_out, *, n_dp, n_tensor,
):
    tokens, model = tokens_in.shape
    width = gate_proj.shape[1]
    heads = step_proj.shape[1]
    head_width = width // heads
    chunks = tokens // T
    seqs = tokens // SEQ_LEN
    per_seq = SEQ_LEN // T
    wide = width + 2 * N
    full = wide + LANES
    inner_width = width * n_tensor

    aux = token_aux(segments)

    projections = (gate_proj, value_proj, state_proj, step_proj.T)
    block = tokens // 4
    lead = 2 * T
    by_rows = lambda columns: pl.BlockSpec((lead, columns), lambda i: (i, 0))
    by_chunks = lambda *shape: pl.BlockSpec((lead // T,) + shape, lambda i: (i, 0, 0))
    held = lambda value: pl.BlockSpec(
        value.shape, lambda i: (0,) * value.ndim, pipeline_mode=pl.Buffered(1)
    )
    vbias = conv_value_bias.reshape(width // LANES, LANES)
    sbias = conv_state_bias.reshape(2 * N // LANES, LANES)
    head_pair = jnp.stack([step_bias, decay_log])
    decay_rate = -jnp.exp(decay_log)
    skip = jnp.repeat(skip_gain, head_width).reshape(width // LANES, LANES)
    gain = norm_gain.reshape(width // LANES, LANES)
    sds = jax.ShapeDtypeStruct
    pg_rows = pre_gain.reshape(model // LANES, LANES)
    consts = (pg_rows,) + projections + (out_proj, conv_value, conv_state, vbias, sbias)
    consts += (head_pair, skip, gain)
    normed, gate_raw, vs_raw, z_raw, grad_normed_out, y, act, pre, stat, sin = pl.pallas_call(
        lead_kernel,
        grid=(tokens // lead,),
        in_specs=[by_rows(model), by_rows(model), by_chunks(16, T)]
        + [held(v) for v in consts],
        out_specs=[by_rows(c) for c in (model, width, wide, LANES, width, width, wide, wide)]
        + [by_chunks(2, T), by_chunks(N, width)],
        out_shape=[
            sds((tokens, model), bf16), sds((tokens, width), bf16), sds((tokens, wide), bf16),
            sds((tokens, LANES), f32), sds((tokens, width), bf16), sds((tokens, width), f32),
            sds((tokens, wide), bf16), sds((tokens, wide), bf16), sds((chunks, 2, T), f32),
            sds((chunks, N, width), bf16),
        ],
        scratch_shapes=[
            pltpu.VMEM((lead + 8, wide), f32), pltpu.VMEM((N, width), f32),
            pltpu.VMEM((lead // T, 3 * T, width), f32), pltpu.VMEM((lead // T, 2, T, LANES), f32),
            pltpu.VMEM((8, LANES), f32), pltpu.VMEM((LANES, width), bf16),
        ],
        name="lead",
    )(tokens_in, grad_out, aux, *consts)

    if n_tensor == 4:
        others = [swap(stat, "tensor", n_tensor, bit) for bit in (1, 2, 3)]
        stat = (stat + others[0]) + (others[1] + others[2])
    else:
        stat = butterfly(stat, "tensor", n_tensor)
    scale = lax.rsqrt(stat[:, 0] / inner_width + eps_value)
    slope_scale = scale * scale * scale * stat[:, 1] / inner_width
    scales = jnp.stack([scale, slope_scale], axis=1)
    steps = tokens // block
    upper = lax.axis_index("tensor") % 2 if n_tensor == 4 else 0
    upper = jnp.reshape(jnp.asarray(upper, jnp.int32), (1,))
    turn = lambda i, u: jnp.where(i < 2, 2 * i + 1 - u[0], 2 * i - 4 + u[0])
    turned = lambda columns: pl.BlockSpec((block, columns), lambda i, u: (turn(i, u), 0))
    kept_spec = lambda columns: pl.BlockSpec(
        (block, columns), lambda i, u: (jnp.maximum(i - steps // 2, 0), 0)
    )
    sent_spec = lambda columns: pl.BlockSpec(
        (block, columns), lambda i, u: (jnp.minimum(i, steps // 2 - 1), 0)
    )
    fixed = lambda rows, columns: pl.BlockSpec((rows, columns), lambda i, u: (0, 0))
    still = lambda value: pl.BlockSpec(
        value.shape, lambda i, u: (0,) * value.ndim, pipeline_mode=pl.Buffered(1)
    )
    halves = [sds((tokens // 2, model), bf16)] * 2
    gate_bf, mix, normed_out, sent, kept, gate_sums = pl.pallas_call(
        middle_kernel,
        grid_spec=pltpu.PrefetchScalarGridSpec(
            num_scalar_prefetch=1,
            grid=(steps,),
            in_specs=[turned(width)] * 4
            + [pl.BlockSpec((block // T, 2, T), lambda i, u: (turn(i, u), 0, 0))]
            + [still(skip), still(gain), still(out_proj)],
            out_specs=[turned(width)] * 3
            + [sent_spec(model), kept_spec(model), fixed(16, width)],
        ),
        out_shape=[sds((tokens, width), bf16)] * 3 + halves + [sds((16, width), f32)],
        name="middle",
    )(upper, gate_raw, grad_normed_out, y, act, scales, skip, gain, out_proj)
    grad_out_proj = dot_tn(normed_out, grad_out).astype(bf16)
    grad_gate_proj = dot_tn(normed, gate_bf).astype(bf16)
    grad_out_proj = lax.psum(grad_out_proj, "dp")
    grad_out_proj = grad_out_proj.astype(f32)
    grad_gate_proj = reduce_rows(grad_gate_proj, "dp", n_dp, f32)

    start = lax.axis_index("tensor") * (tokens // n_tensor)
    own = lambda v: lax.dynamic_slice_in_dim(v, start, tokens // n_tensor, 0)
    if n_tensor == 4:
        block_out = sum_quarters(kept, sent, (tokens_in,), (), block_kernel)
        block_out = gather_rows(block_out, "tensor", n_tensor, bf16, mixed=True)
    else:
        branch = scatter_halves(kept, sent, "tensor", n_tensor)
        block_out = (own(tokens_in).astype(f32) + branch).astype(bf16)
        block_out = lax.all_gather(block_out, "tensor", axis=0, tiled=True)

    consts = (conv_value, conv_state, head_pair, skip)
    given = (mix, y, act, pre, vs_raw, z_raw, sin, aux)
    out = [sds((tokens, full), bf16), sds((8 * (K + 2), wide), f32)]

    def of(value):
        row = lambda i, j: i * per_seq + per_seq - 1 - j
        if len(value.shape) == 2:
            return pl.BlockSpec((T, value.shape[1]), lambda i, j: (row(i, j), 0))
        return pl.BlockSpec((1,) + value.shape[1:], lambda i, j: (row(i, j), 0, 0))

    def whole(value):
        return pl.BlockSpec(value.shape, lambda i, j: (0, 0), pipeline_mode=pl.Buffered(1))

    packed, csum = pl.pallas_call(
        backward_kernel,
        grid=(seqs, per_seq),
        in_specs=[of(v) for v in given] + [whole(v) for v in consts],
        out_specs=[of(out[0]), pl.BlockSpec(out[1].shape, lambda i, j: (0, 0))],
        out_shape=out,
        scratch_shapes=[
            pltpu.VMEM((N, width), f32), pltpu.VMEM((T + 8, wide), f32),
            pltpu.VMEM((3 * T, width), f32), pltpu.VMEM((T, width), bf16),
            pltpu.VMEM((T, width), bf16), pltpu.VMEM((8, LANES), f32),
            pltpu.VMEM((8, LANES), f32), pltpu.VMEM((5, T, width), bf16),
            pltpu.VMEM((LANES, width), bf16), pltpu.VMEM((width, LANES), bf16),
        ],
        name="ssd_backward",
    )(*given, *consts)

    grad_packed = dot_tn(normed, packed).astype(bf16)
    grad_value_proj = grad_packed[:, :width]
    grad_state_proj = grad_packed[:, width:wide]
    grad_step_proj = grad_packed[:, wide : wide + heads].T
    sent, kept, gain_part = pl.pallas_call(
        group_kernel,
        grid_spec=pltpu.PrefetchScalarGridSpec(
            num_scalar_prefetch=1,
            grid=(steps,),
            in_specs=[turned(width), turned(full), turned(model)]
            + [still(w) for w in projections],
            out_specs=[sent_spec(model), kept_spec(model), fixed(8, model)],
            scratch_shapes=[pltpu.VMEM((block, model), bf16)],
        ),
        out_shape=halves + [sds((8, model), f32)],
        name="group_in",
    )(upper, gate_bf, packed, normed, *projections)
    gate_sums = jnp.pad(gate_sums, ((0, 0), (0, 2 * N)))
    sums = jnp.sum(jnp.concatenate([csum, gate_sums]).reshape(K + 4, 8, wide), axis=1)
    gain_part = jnp.sum(gain_part, axis=0) / pre_gain

    grad_value_proj = reduce_rows(grad_value_proj, "dp", n_dp, f32)

    if n_tensor == 4:
        gain_row = pre_gain[None, :]
        grad_in = sum_quarters(kept, sent, (tokens_in, grad_out), (gain_row,), input_kernel)
    else:
        grad_normed = scatter_halves(kept, sent, "tensor", n_tensor)
        own_hidden = own(tokens_in).astype(f32)
        own_inv = lax.rsqrt(jnp.mean(own_hidden * own_hidden, axis=1, keepdims=True) + eps_value)
        weighted = pre_gain * grad_normed
        grad_hidden = own_inv * weighted - own_hidden * (own_inv * own_inv * own_inv) * jnp.mean(
            weighted * own_hidden, axis=1, keepdims=True
        )
        grad_in = (own(grad_out).astype(f32) + grad_hidden).astype(bf16)
    grad_in = lax.all_gather(grad_in, "tensor", axis=0, tiled=True)
    grad_in = copy_rows(grad_in)

    gain_rows = model // (2 * N)
    extra = jnp.concatenate([sums[:, width:], gain_part.reshape(gain_rows, 2 * N)], axis=0)
    unit = n_tensor * math.lcm(16, model // math.gcd(model, 2 * N))
    gap = -(model + extra.shape[0]) % unit
    extra = jnp.pad(extra, ((0, gap), (0, 0))).astype(bf16)
    shared = jnp.concatenate([grad_state_proj, extra], axis=0)
    shared = scatter_sum(shared, "tensor", n_tensor).astype(bf16)
    small = jnp.concatenate([jnp.pad(sums, ((0, 0), (0, model - wide))), grad_step_proj], axis=0)
    part = shared.shape[0]
    flat = part * 2 * N // model
    both = jnp.concatenate([shared.reshape(flat, model), small.astype(bf16)], axis=0)
    both = butterfly(both, "dp", n_dp)
    shared, small = both[:flat].reshape(part, 2 * N), both[flat:].astype(f32)
    shared = gather_rows(shared, "tensor", n_tensor, bf16)
    grad_state_proj = shared[:model].astype(f32)
    state_sums = shared[model : model + K + 4].astype(f32)
    grad_pre_gain = shared[model + K + 4 : model + K + 4 + gain_rows].reshape(model).astype(f32)
    sums = small[: K + 4]
    grad_step_proj = small[K + 4 :].T
    grad_skip = jnp.sum(sums[K + 3, :width].reshape(heads, head_width), axis=1)
    return (
        block_out,
        grad_in,
        grad_pre_gain,
        grad_gate_proj,
        grad_value_proj,
        grad_state_proj,
        grad_step_proj,
        sums[:K, :width],
        sums[K, :width],
        state_sums[:K],
        state_sums[K],
        sums[K + 1, :heads],
        sums[K + 1, LANES : LANES + heads] * decay_rate,
        grad_skip,
        sums[K + 2, :width],
        grad_out_proj,
    )


def solution(mesh):
    t = P("tensor")
    cols = P(None, "tensor")
    in_specs = (
        P("dp", None), P("dp"), P(), cols, cols, P(), cols, cols, t, P(), P(), t, t, t, t,
        P("tensor", None), P("dp", None),
    )
    out_specs = (
        P("dp", None), P("dp", None), P(), cols, cols, P(), cols, cols, t, P(), P(), t, t, t, t,
        P("tensor", None),
    )
    n_dp, n_tensor = mesh.shape["dp"], mesh.shape["tensor"]

    def body(*args):
        return on_device(*args, n_dp=n_dp, n_tensor=n_tensor)

    return jax.shard_map(body, mesh=mesh, in_specs=in_specs, out_specs=out_specs, check_vma=False)
```

```python
import math

import jax
import jax.numpy as jnp
from jax import lax
from jax.experimental import pallas as pl
from jax.experimental.pallas import tpu as pltpu
from jax.sharding import PartitionSpec as P


N = 128
K = 4
SEQ_LEN = 1024
T = 128
LANES = 128
HALF = 64
NEG = -1e30
eps_value = 1e-05
f32 = jnp.float32
bf16 = jnp.bfloat16


def dot(a, b):
    return jnp.dot(a, b, preferred_element_type=f32)


def dot_nt(a, b):
    return lax.dot_general(a, b, (((1,), (1,)), ((), ())), preferred_element_type=f32)


def dot_tn(a, b):
    return lax.dot_general(a, b, (((0,), (0,)), ((), ())), preferred_element_type=f32)


def sigmoid(v):
    return 0.5 * jnp.tanh(0.5 * v) + 0.5


def two_terms(v):
    high = v.astype(bf16)
    return high, (v - high.astype(f32)).astype(bf16)


def paired(v):
    high, low = two_terms(v)
    lane = lax.broadcasted_iota(jnp.int32, v.shape, 1)
    return jnp.where(lane < HALF, high, low)


def sum_rows(v):
    total = v[0:8]
    for row in range(8, v.shape[0], 8):
        total = total + v[row : row + 8]
    return total


def head_rows(heads_ref, lane_ref):
    count = heads_ref.shape[1]
    lane_ref[...] = jnp.zeros_like(lane_ref)
    lane_ref[0:2, 0:count] = heads_ref[...]
    lane_ref[0:2, HALF : HALF + count] = heads_ref[...]
    return lane_ref[0:1, :], -jnp.exp(lane_ref[1:2, :])


def ones_where(condition):
    return jnp.where(condition, 1.0, 0.0).astype(bf16)


def expansion(shape, head_width):
    lane = lax.broadcasted_iota(jnp.int32, shape, 0)
    owner = lax.broadcasted_iota(jnp.int32, shape, 1) // head_width
    return ones_where((lane == owner) | (lane == owner + HALF))


def reduction(shape, head_width):
    owner = lax.broadcasted_iota(jnp.int32, shape, 0) // head_width
    return ones_where(lax.broadcasted_iota(jnp.int32, shape, 1) == owner)


def triangle():
    row = lax.broadcasted_iota(jnp.int32, (T, T), 0)
    col = lax.broadcasted_iota(jnp.int32, (T, T), 1)
    return row, col


def head_terms(z_ref, bias, rate, aux, tri, e_ref, ex_ref):
    z = z_ref[...] + bias
    tail = jnp.exp(-jnp.abs(z))
    step = jnp.maximum(z, 0.0) + jnp.log1p(tail)
    high, low = two_terms(step * rate)
    cum = dot(tri, high) + dot(tri, low)
    end = cum[T - 1 : T]
    dst = jnp.exp(cum) * aux[:, 3:4]
    dend = jnp.exp(end - cum) * aux[:, 4:5]
    total = jnp.exp(jnp.broadcast_to(end, (8, LANES))) * aux[T - 1 : T, 3:4]
    stacked = jnp.concatenate([paired(step), paired(dend), paired(dst)], axis=0)
    ex_ref[...] = dot(stacked, e_ref[...])
    carry = dot(paired(total), e_ref[...])[0:1]
    return z, step, cum, cum.T, carry


def taps_of(c, width, vtaps_ref, staps_ref):
    ref, at = (vtaps_ref, c) if c.start < width else (staps_ref, slice(c.start - width, c.stop - width))
    return lambda s: ref[K - 1 - s : K - s, at]


def lead_kernel(
    tokens_ref, go_ref, aux_ref, pg_ref, gate_w, value_w, state_w, step_w, out_w,
    vtaps_ref, staps_ref, vbias_ref, sbias_ref, heads_ref, skip_ref, ng_ref,
    normed_ref, gate_ref, vs_ref, z_ref, gno_ref, y_ref, act_ref, pre_ref, stat_ref, sin_ref,
    ext_ref, state_ref, ex_ref, sum_ref, lane_ref, e_ref,
):
    rows, width = gate_ref.shape
    chunks = range(rows // T)

    @pl.when(pl.program_id(0) == 0)
    def _():
        e_ref[...] = expansion(e_ref.shape, width // heads_ref.shape[1])

    @pl.when(pl.program_id(0) % (SEQ_LEN // rows) == 0)
    def _():
        state_ref[...] = jnp.zeros_like(state_ref)
        ext_ref[0:8, :] = jnp.zeros_like(ext_ref[0:8, :])

    part = 32

    def normalize(index, carry):
        r = pl.ds(pl.multiple_of(index * part, part), part)
        hidden = tokens_ref[r, :].astype(f32)
        inv = lax.rsqrt(jnp.mean(hidden * hidden, axis=1, keepdims=True) + eps_value)
        for k in range(pg_ref.shape[0]):
            c = slice(k * LANES, (k + 1) * LANES)
            normed_ref[r, c] = (hidden[:, c] * inv * pg_ref[k : k + 1, :]).astype(bf16)
        return carry

    lax.fori_loop(0, rows // part, normalize, 0)
    z = dot_nt(normed_ref[...], step_w[...])
    z_ref[...] = jnp.zeros_like(z_ref)
    z_ref[:, : z.shape[1]] = z
    z_ref[:, HALF : HALF + z.shape[1]] = z
    raw = dot(normed_ref[...], state_w[...])
    ext_ref[8:, width:] = raw
    vs_ref[:, width:] = raw.astype(bf16)
    at = [pl.ds(k * T, T) for k in chunks]
    bias, rate = head_rows(heads_ref, lane_ref)
    row, col = triangle()
    tri = ones_where(row >= col)
    aux = [aux_ref[k].T for k in chunks]
    terms = [
        head_terms(z_ref.at[at[k]], bias, rate, aux[k], tri, e_ref, ex_ref.at[k])
        for k in chunks
    ]
    keep = [
        [jnp.broadcast_to(aux[k][:, s : s + 1], (T, LANES)) for s in range(K - 1)] for k in chunks
    ]

    def activate(c, k):
        lo = 8 + k * T
        tap, shift = taps_of(c, width, vtaps_ref, staps_ref), c.start // LANES
        if c.start < width:
            pre = vbias_ref[shift : shift + 1, :]
        else:
            pre = sbias_ref[shift - width // LANES : shift - width // LANES + 1, :]
        pre = pre + tap(0) * ext_ref[lo : lo + T, c]
        for s in range(1, K):
            pre = pre + tap(s) * (ext_ref[lo - s : lo - s + T, c] * keep[k][s - 1])
        half = 0.5 * pre
        act = half + half * jnp.tanh(half)
        act_bf = act.astype(bf16)
        pre_ref[at[k], c] = pre.astype(bf16)
        act_ref[at[k], c] = act_bf
        return act, act_bf

    b_flip, c_mats, scores, fades = [], [], [], []
    for k in chunks:
        _, b_mat = activate(slice(width, width + N), k)
        _, c_mat = activate(slice(width + N, width + 2 * N), k)
        b_flip.append(b_mat.T)
        c_mats.append(c_mat)
        scores.append(dot_nt(c_mat, b_mat))
        same = (aux[k][:, 5:6] == aux_ref[k, 5:6, :]) & (row >= col)
        fades.append(jnp.where(same, 0.0, NEG))
    first = lax.broadcasted_iota(jnp.int32, (T, LANES), 1) < HALF
    sum_ref[...] = jnp.zeros_like(sum_ref)
    span = 2 * LANES if width % (2 * LANES) == 0 else LANES
    for lo in range(0, width, span):
        group = slice(lo, lo + span)
        raw = dot(normed_ref[...], value_w[:, group])
        ext_ref[8:, group] = raw
        vs_ref[:, group] = raw.astype(bf16)
        gates = dot(normed_ref[...], gate_w[:, group])
        gate_ref[:, group] = gates.astype(bf16)
        gnos = dot_nt(go_ref[...], out_w[group, :])
        gno_ref[:, group] = gnos.astype(bf16)
        for pair in range(lo // LANES, (lo + span) // LANES):
            c = slice(pair * LANES, (pair + 1) * LANES)
            inside = slice(pair * LANES - lo, (pair + 1) * LANES - lo)
            for k in chunks:
                _, _, cum, cum_t, carry = terms[k]
                r = slice(k * T, (k + 1) * T)
                act, act_bf = activate(c, k)
                xt_full = act_bf.astype(f32) * ex_ref[k, 0:T, c]
                xt = xt_full.astype(bf16)
                xd = (xt_full * ex_ref[k, T : 2 * T, c]).astype(bf16)
                mixes = []
                for h in (2 * pair, 2 * pair + 1):
                    decay = jnp.exp(fades[k] + (cum[:, h : h + 1] - cum_t[h : h + 1, :]))
                    mixes.append((scores[k] * decay).astype(bf16))
                zero = jnp.zeros_like(xt)
                blocks = [jnp.where(first, xt, zero), jnp.where(first, zero, xt)]
                state = state_ref[:, c]
                state_bf = state.astype(bf16)
                sin_ref[k, :, c] = state_bf
                y = dot(jnp.concatenate(mixes, axis=1), jnp.concatenate(blocks, axis=0))
                y = y + ex_ref[k, 2 * T : 3 * T, c] * dot(c_mats[k], state_bf)
                y_ref[r, c] = y
                state_ref[:, c] = state * carry[:, c] + dot(b_flip[k], xd)
                half = 0.5 * gates[r, inside]
                gated = (y + skip_ref[pair : pair + 1, :] * act) * (half + half * jnp.tanh(half))
                sum_ref[k, 0] += gated * gated
                sum_ref[k, 1] += gated * ng_ref[pair : pair + 1, :] * gnos[r, inside]
    for k in chunks:
        for s in range(2):
            stat_ref[k, s : s + 1, :] = jnp.sum(sum_ref[k, s].T, axis=0, keepdims=True)
    ext_ref[0:8, :] = ext_ref[rows : rows + 8, :]


def store_half(value, sent_ref, kept_ref):
    first = pl.program_id(0) < pl.num_programs(0) // 2

    @pl.when(first)
    def _():
        sent_ref[...] = value

    @pl.when(jnp.logical_not(first))
    def _():
        kept_ref[...] = value


def middle_kernel(
    _, gate_ref, gno_ref, y_ref, act_ref, stat_ref, skip_ref, ng_ref, out_w,
    gate_grad_ref, mix_ref, normed_ref, sent_ref, kept_ref, csum_ref,
):
    @pl.when(pl.program_id(0) == 0)
    def _():
        csum_ref[...] = jnp.zeros_like(csum_ref)

    def one(chunk, carry):
        r = pl.ds(pl.multiple_of(chunk * T, T), T)
        scale = jnp.broadcast_to(stat_ref[chunk, 0:1, :], (LANES, T)).T
        slope_scale = jnp.broadcast_to(stat_ref[chunk, 1:2, :], (LANES, T)).T
        for pair in range(gate_ref.shape[1] // LANES):
            c = slice(pair * LANES, (pair + 1) * LANES)
            gate = gate_ref[r, c].astype(f32)
            logistic = sigmoid(gate)
            swish = gate * logistic
            x = act_ref[r, c].astype(f32)
            gno = gno_ref[r, c].astype(f32)
            ssd = y_ref[r, c] + skip_ref[pair : pair + 1, :] * x
            gated = ssd * swish
            unit = gated * scale
            normed_ref[r, c] = (unit * ng_ref[pair : pair + 1, :]).astype(bf16)
            grad_gated = scale * (gno * ng_ref[pair : pair + 1, :]) - slope_scale * gated
            csum_ref[0:8, c] += sum_rows(gno * unit)
            grad_mix = grad_gated * swish
            grad_gate = grad_gated * ssd * (logistic + swish * (1.0 - logistic))
            gate_grad_ref[r, c] = grad_gate.astype(bf16)
            csum_ref[8:16, c] += sum_rows(grad_mix * x)
            mix_ref[r, c] = grad_mix.astype(bf16)
        return carry

    lax.fori_loop(0, stat_ref.shape[0], one, 0)
    store_half(dot(normed_ref[...], out_w[...]).astype(bf16), sent_ref, kept_ref)


def backward_kernel(
    mix_ref, y_ref, act_ref, pre_ref, vs_ref, z_ref, sin_ref, aux_ref,
    vtaps_ref, staps_ref, heads_ref, skip_ref,
    grad_ref, csum_ref,
    back_ref, ext_ref, ex_ref, xd_ref, gd_ref, through_ref, lane_ref, part_ref, e_ref, er_ref,
):
    width = mix_ref.shape[1]

    @pl.when((pl.program_id(0) == 0) & (pl.program_id(1) == 0))
    def _():
        csum_ref[...] = jnp.zeros_like(csum_ref)
        e_ref[...] = expansion(e_ref.shape, width // heads_ref.shape[1])
        er_ref[...] = reduction(er_ref.shape, width // heads_ref.shape[1])

    @pl.when(pl.program_id(1) == 0)
    def _():
        back_ref[...] = jnp.zeros_like(back_ref)
        ext_ref[T : T + 8, :] = jnp.zeros_like(ext_ref[T : T + 8, :])

    row, col = triangle()
    tri, triu = ones_where(row >= col), ones_where(row <= col)
    bias, rate = head_rows(heads_ref, lane_ref)
    aux = aux_ref[0].T
    z, step, cum, cum_t, carry = head_terms(z_ref, bias, rate, aux, tri, e_ref, ex_ref)
    keep = [jnp.broadcast_to(aux[:, 5 + s : 6 + s], (T, LANES)) for s in range(1, K)]
    b_mat = act_ref[:, width : width + N]
    c_mat = act_ref[:, width + N : width + 2 * N]
    scores_t = dot_nt(b_mat, c_mat)
    same = (aux[:, 5:6] == aux_ref[0, 5:6, :]) & (row <= col)
    fade = jnp.where(same, 0.0, NEG)
    lane = lax.broadcasted_iota(jnp.int32, (T, LANES), 1)
    first = lane < HALF
    back_bf = back_ref[...].astype(bf16)

    def conv_back(grad_pre, c):
        ext_ref[0:T, c] = grad_pre
        raw = vs_ref[:, c].astype(f32)
        tap = taps_of(c, width, vtaps_ref, staps_ref)
        grad_raw = tap(0) * grad_pre
        csum_ref[8 * (K - 1) : 8 * K, c] += sum_rows(grad_pre * raw)
        csum_ref[8 * K : 8 * K + 8, c] += sum_rows(grad_pre)
        for s in range(1, K):
            moved = ext_ref[s : s + T, c] * keep[s - 1]
            grad_raw = grad_raw + tap(s) * moved
            csum_ref[8 * (K - 1 - s) : 8 * (K - s), c] += sum_rows(moved * raw)
        return grad_raw

    def slope(c):
        pre = pre_ref[:, c].astype(f32)
        logistic = sigmoid(pre)
        return logistic * (1.0 + pre * (1.0 - logistic))

    def through_of(value):
        high, low = two_terms(sum_rows(value))
        through = dot(high, er_ref[...]) + dot(low, er_ref[...])
        return jnp.broadcast_to(jnp.sum(through, axis=0, keepdims=True), (8, LANES))

    grad_scores = jnp.zeros((T, T), f32)
    through_ref[...] = through_of(sin_ref[0].astype(f32) * back_ref[...] * carry)
    for pair in range(width // LANES):
        c = slice(pair * LANES, (pair + 1) * LANES)
        x = act_ref[:, c].astype(f32)
        y = y_ref[:, c]
        g = mix_ref[:, c]
        grad_mix = g.astype(f32)
        step_x = ex_ref[0:T, c]
        dend_x = ex_ref[T : 2 * T, c]
        gd_ref[:, c] = (grad_mix * ex_ref[2 * T : 3 * T, c]).astype(bf16)
        xt_full = x * step_x
        xt = xt_full.astype(bf16)
        xd_ref[:, c] = (xt_full * dend_x).astype(bf16)
        zero = jnp.zeros_like(g)
        g_blocks = jnp.concatenate([jnp.where(first, g, zero), jnp.where(first, zero, g)], axis=0)
        x_blocks = jnp.concatenate([jnp.where(first, xt, zero), jnp.where(first, zero, xt)], axis=0)
        products = dot_nt(x_blocks, g)
        mixes = []
        for k, h in enumerate((2 * pair, 2 * pair + 1)):
            decay = jnp.exp(fade + (cum_t[h : h + 1, :] - cum[:, h : h + 1]))
            mixes.append((scores_t * decay).astype(bf16))
            grad_scores = grad_scores + products[k * T : (k + 1) * T] * decay
        u_in = dot(jnp.concatenate(mixes, axis=1), g_blocks)
        u_far = dend_x * dot(b_mat, back_bf[:, c])
        u = u_in + u_far
        y_far = ex_ref[2 * T : 3 * T, c] * dot(c_mat, sin_ref[0, :, c])
        xt_wide = xt.astype(f32)
        part_ref[0, :, c], part_ref[1, :, c] = two_terms(grad_mix * (y - y_far) - xt_wide * u_in)
        part_ref[2, :, c] = (grad_mix * y_far).astype(bf16)
        part_ref[3, :, c] = (xt_wide * u_far).astype(bf16)
        part_ref[4, :, c] = (x * u).astype(bf16)
        grad_value = step_x * u + skip_ref[pair : pair + 1, :] * grad_mix
        grad_ref[:, c] = conv_back(grad_value * slope(c), c).astype(bf16)

    gs_bf = grad_scores.astype(bf16)
    grad_b = dot(gs_bf, c_mat) + dot_nt(xd_ref[...], back_bf)
    grad_c = dot_tn(gs_bf, b_mat) + dot_nt(gd_ref[...], sin_ref[0])
    for k, grad in enumerate((grad_b, grad_c)):
        c = slice(width + k * N, width + (k + 1) * N)
        grad_ref[:, c] = conv_back(grad * slope(c), c).astype(bf16)
    ext_ref[T : T + 8, :] = ext_ref[0:8, :]

    by_head = [dot(part_ref[k], er_ref[...]) for k in range(5)]
    col_far, direct = by_head[3:]
    high, low = two_terms(by_head[0] + by_head[1] + by_head[2])
    grad_acc = through_ref[0:1, :] + (dot(triu, high) + dot(triu, low))
    high, low = two_terms(col_far)
    grad_acc = grad_acc + (dot(tri, high) + dot(tri, low)) - col_far
    grad_step = direct + grad_acc * rate
    grad_z = grad_step * sigmoid(z)
    csum_ref[8 * (K + 1) : 8 * (K + 2), 0:LANES] += sum_rows(grad_z)
    csum_ref[8 * (K + 1) : 8 * (K + 2), LANES : 2 * LANES] += sum_rows(grad_acc * step)
    grad_ref[:, width + 2 * N :] = grad_z.astype(bf16)

    new_back = back_ref[...] * carry + dot_tn(c_mat, gd_ref[...])
    back_ref[...] = new_back


def bits_of(size):
    return [1 << k for k in range(size.bit_length() - 1)] if size & (size - 1) == 0 else None


def swap(value, axis, size, bit):
    return lax.ppermute(value, axis, [(i, i ^ bit) for i in range(size)])


def block_of(rows):
    return max(b for b in range(16, 513, 16) if rows % b == 0)


def place(buffer, value, slot, dtype, parts):
    rows, width = value.shape
    block = block_of(rows)
    count = rows // block

    def kernel(slot_ref, value_ref, *refs):
        refs[-1][...] = value_ref[...].astype(dtype)

    out = jax.ShapeDtypeStruct((parts * rows, width), dtype)
    given = () if buffer is None else (buffer,)
    return pl.pallas_call(
        kernel,
        grid_spec=pltpu.PrefetchScalarGridSpec(
            num_scalar_prefetch=1,
            grid=(count,),
            in_specs=[pl.BlockSpec((block, width), lambda i, s: (i, 0))]
            + [pl.BlockSpec(memory_space=pl.ANY) for _ in given],
            out_specs=pl.BlockSpec((block, width), lambda i, s: (s[0] * count + i, 0)),
        ),
        out_shape=out,
        input_output_aliases={2: 0} if given else {},
        name="place",
    )(jnp.reshape(slot, (1,)).astype(jnp.int32), value, *given)


def copy_rows(value):
    def kernel(value_ref, out_ref):
        out_ref[...] = value_ref[...]

    spec = pl.BlockSpec((block_of(value.shape[0]), value.shape[1]), lambda i: (i, 0))
    return pl.pallas_call(
        kernel,
        grid=(value.shape[0] // spec.block_shape[0],),
        in_specs=[spec],
        out_specs=spec,
        out_shape=jax.ShapeDtypeStruct(value.shape, value.dtype),
        name="copy_rows",
    )(value)


def assemble(pieces, slots, dtype):
    rows, width = pieces[0].shape

    def kernel(slots_ref, *refs):
        for k, ref in enumerate(refs[:-1]):

            @pl.when(pl.program_id(0) == k)
            def _(ref=ref):
                refs[-1][...] = ref[...].astype(dtype)

    return pl.pallas_call(
        kernel,
        grid_spec=pltpu.PrefetchScalarGridSpec(
            num_scalar_prefetch=1,
            grid=(len(pieces),),
            in_specs=[pl.BlockSpec((rows, width), lambda i, s: (0, 0)) for _ in pieces],
            out_specs=pl.BlockSpec((rows, width), lambda i, s: (s[i], 0)),
        ),
        out_shape=jax.ShapeDtypeStruct((len(pieces) * rows, width), dtype),
        name="assemble",
    )(jnp.stack(slots).astype(jnp.int32), *pieces)


def join(value, other, upper):
    rows, width = value.shape
    block = block_of(rows)
    count = rows // block

    def kernel(upper_ref, value_ref, other_ref, out_ref):
        mine = pl.program_id(0) == upper_ref[0]

        @pl.when(mine)
        def _():
            out_ref[...] = value_ref[...]

        @pl.when(jnp.logical_not(mine))
        def _():
            out_ref[...] = other_ref[...]

    return pl.pallas_call(
        kernel,
        grid_spec=pltpu.PrefetchScalarGridSpec(
            num_scalar_prefetch=1,
            grid=(2, count),
            in_specs=[
                pl.BlockSpec((block, width), lambda h, i, u: (jnp.where(h == u[0], i, 0), 0)),
                pl.BlockSpec((block, width), lambda h, i, u: (jnp.where(h == u[0], 0, i), 0)),
            ],
            out_specs=pl.BlockSpec((block, width), lambda h, i, u: (h * count + i, 0)),
        ),
        out_shape=jax.ShapeDtypeStruct((2 * rows, width), value.dtype),
        name="join",
    )(jnp.reshape(upper, (1,)).astype(jnp.int32), value, other)


def add_parts(parts, start, rows):
    total = None
    for value, base in parts:
        piece = lax.dynamic_slice_in_dim(value, base + start, rows, 0).astype(f32)
        total = piece if total is None else total + piece
    return total


def sum_quarters(kept, sent, arrays, rows, kernel):
    index = lax.axis_index("tensor")
    other = swap(sent, "tensor", 4, 1)
    upper = index // 2
    quarter, width = kept.shape[0] // 2, kept.shape[1]
    out = add_parts([(kept, 0), (other, 0)], (1 - upper) * quarter, quarter).astype(kept.dtype)
    last = swap(out, "tensor", 4, 2)
    count = quarter // T
    half = pl.BlockSpec((T, width), lambda i, s: (s[1] * count + i, 0))
    own = pl.BlockSpec((T, width), lambda i, s: (s[0] * count + i, 0))
    plain = pl.BlockSpec((T, width), lambda i, s: (i, 0))
    return pl.pallas_call(
        kernel,
        grid_spec=pltpu.PrefetchScalarGridSpec(
            num_scalar_prefetch=1,
            grid=(count,),
            in_specs=[half, half, plain]
            + [own for _ in arrays]
            + [pl.BlockSpec(v.shape, lambda i, s: (0, 0)) for v in rows],
            out_specs=plain,
        ),
        out_shape=jax.ShapeDtypeStruct((quarter, width), bf16),
        name="quarter",
    )(jnp.stack([index, upper]).astype(jnp.int32), kept, other, last, *arrays, *rows)


def block_kernel(_, kept_ref, other_ref, last_ref, tokens_ref, out_ref):
    total = kept_ref[...].astype(f32) + other_ref[...].astype(f32) + last_ref[...].astype(f32)
    out_ref[...] = (tokens_ref[...].astype(f32) + total).astype(bf16)


def input_kernel(_, kept_ref, other_ref, last_ref, tokens_ref, grad_ref, gain_ref, out_ref):
    part = 32

    def one(index, carry):
        r = pl.ds(pl.multiple_of(index * part, part), part)
        total = kept_ref[r, :].astype(f32) + other_ref[r, :].astype(f32) + last_ref[r, :].astype(f32)
        hidden = tokens_ref[r, :].astype(f32)
        inv = lax.rsqrt(jnp.mean(hidden * hidden, axis=1, keepdims=True) + eps_value)
        weighted = gain_ref[0:1, :] * total
        mean = jnp.mean(weighted * hidden, axis=1, keepdims=True)
        grad_hidden = inv * weighted - hidden * (inv * inv * inv * mean)
        out_ref[r, :] = (grad_ref[r, :].astype(f32) + grad_hidden).astype(bf16)
        return carry

    lax.fori_loop(0, out_ref.shape[0] // part, one, 0)


def scatter_halves(kept, sent, axis, size):
    bits = bits_of(size)
    if size != 4:
        quarter = (2, kept.shape[0] // 2, kept.shape[1])
        value = jnp.stack([kept.reshape(quarter), sent.reshape(quarter)], axis=1)
        value = value.reshape(2 * kept.shape[0], kept.shape[1])
        return lax.psum_scatter(value, axis, scatter_dimension=0, tiled=True).astype(f32)
    other = swap(sent, axis, size, bits[0])
    return scatter_parts([(kept, 0), (other, 0)], axis, size, bits[1:])


def scatter_sum(value, axis, size):
    bits = bits_of(size)
    if bits is None:
        return lax.psum_scatter(value, axis, scatter_dimension=0, tiled=True).astype(f32)
    return scatter_parts([(value, 0)], axis, size, bits)


def scatter_parts(parts, axis, size, bits):
    index = lax.axis_index(axis)
    value = parts[0][0]
    rows = value.shape[0]
    for bit in bits:
        upper = (index // bit) % 2
        rows = rows // 2
        sent = add_parts(parts, (1 - upper) * rows, rows).astype(value.dtype)
        other = swap(sent, axis, size, bit)
        parts = [(part, base + upper * rows) for part, base in parts] + [(other, 0)]
    return add_parts(parts, 0, rows)


def rows_are_few(value):
    return value.size * value.dtype.itemsize < 2**18


def gather_rows(value, axis, size, dtype, mixed=False):
    index = lax.axis_index(axis)
    bits = bits_of(size)
    if bits is None or len(bits) < 2:
        return lax.all_gather(value, axis, axis=0, tiled=True).astype(dtype)
    for bit in bits[:1:-1]:
        other = swap(value, axis, size, bit)
        value = join(value, other, (index // bit) % 2)
    outer, inner = bits[:2]
    near = swap(value, axis, size, inner)
    far = swap(value, axis, size, outer)
    both = swap(near, axis, size, outer)
    side, half = (index // outer) % 2, (index // inner) % 2

    def slot(flip_outer, flip_inner):
        x, y = (1 - side if flip_outer else side), (1 - half if flip_inner else half)
        return x + 2 * y if mixed else 2 * x + y

    if rows_are_few(value):
        pieces = (value, far, near, both)
        return assemble(pieces, [slot(0, 0), slot(1, 0), slot(0, 1), slot(1, 1)], dtype)
    buffer = None
    for piece, flips in ((value, (0, 0)), (far, (1, 0)), (near, (0, 1)), (both, (1, 1))):
        buffer = place(buffer, piece, slot(*flips), dtype, 4)
    return buffer


def reduce_rows(value, axis, size, dtype):
    part = scatter_sum(value, axis, size).astype(value.dtype)
    return gather_rows(part, axis, size, dtype)


def butterfly(value, axis, size):
    bits = bits_of(size)
    if bits is None:
        return lax.psum(value, axis)
    for bit in bits:
        value = value + swap(value, axis, size, bit)
    return value


def token_aux(segments):
    count = segments.shape[0]
    seg = segments.astype(f32)
    position = jnp.arange(count, dtype=jnp.int32) % SEQ_LEN
    columns = []
    lifted = []
    for s in range(1, K):
        before = jnp.concatenate([jnp.zeros((s,), f32), seg[:-s]])
        keep = ((position >= s) & (seg == before)).astype(f32)
        columns.append(keep)
        lifted.append(jnp.concatenate([keep[s:], jnp.zeros((s,), f32)]))
    chunked = seg.reshape(count // T, T)
    last = chunked[:, T - 1]
    starts = (jnp.arange(count // T, dtype=jnp.int32) * T) % SEQ_LEN == 0
    before = jnp.where(starts, -1.0, jnp.concatenate([jnp.zeros((1,), f32), last[:-1]]))
    columns.append((chunked == before[:, None]).astype(f32).reshape(count))
    columns.append((chunked == last[:, None]).astype(f32).reshape(count))
    columns.append(seg)
    rows = [row.reshape(count // T, T) for row in columns + lifted]
    return jnp.stack(rows + [rows[0]] * (16 - len(rows)), axis=1)


def group_kernel(
    _, gate_ref, packed_ref, normed_ref, gate_w, value_w, state_w, step_w,
    sent_ref, kept_ref, gain_ref, in_ref,
):
    weights = (value_w, state_w)
    steps = packed_ref[:, value_w.shape[1] + state_w.shape[1] :][:, : step_w.shape[0]]

    @pl.when(pl.program_id(0) == 0)
    def _():
        gain_ref[...] = jnp.zeros_like(gain_ref)

    model = in_ref.shape[1]
    part = model // 3 if model % 384 == 0 else model

    def one(index, carry):
        c = pl.ds(pl.multiple_of(index * part, part), part)
        total, at = dot_nt(gate_ref[...], gate_w[c, :]) + dot(steps, step_w[:, c]), 0
        for w in weights:
            total = total + dot_nt(packed_ref[:, at : at + w.shape[1]], w[c, :])
            at += w.shape[1]
        rounded = total.astype(bf16)
        in_ref[:, c] = rounded
        gain_ref[:, c] += sum_rows(rounded.astype(f32) * normed_ref[:, c].astype(f32))
        return carry

    lax.fori_loop(0, model // part, one, 0)
    store_half(in_ref[...], sent_ref, kept_ref)


def on_device(
    tokens_in, segments, pre_gain, gate_proj, value_proj, state_proj, step_proj, conv_value,
    conv_value_bias, conv_state, conv_state_bias, step_bias, decay_log, skip_gain, norm_gain,
    out_proj, grad_out, *, n_dp, n_tensor,
):
    tokens, model = tokens_in.shape
    width = gate_proj.shape[1]
    heads = step_proj.shape[1]
    head_width = width // heads
    chunks = tokens // T
    seqs = tokens // SEQ_LEN
    per_seq = SEQ_LEN // T
    wide = width + 2 * N
    full = wide + LANES
    inner_width = width * n_tensor

    aux = token_aux(segments)

    projections = (gate_proj, value_proj, state_proj, step_proj.T)
    block = tokens // 4
    lead = 2 * T
    by_rows = lambda columns: pl.BlockSpec((lead, columns), lambda i: (i, 0))
    by_chunks = lambda *shape: pl.BlockSpec((lead // T,) + shape, lambda i: (i, 0, 0))
    held = lambda value: pl.BlockSpec(
        value.shape, lambda i: (0,) * value.ndim, pipeline_mode=pl.Buffered(1)
    )
    vbias = conv_value_bias.reshape(width // LANES, LANES)
    sbias = conv_state_bias.reshape(2 * N // LANES, LANES)
    head_pair = jnp.stack([step_bias, decay_log])
    decay_rate = -jnp.exp(decay_log)
    skip = jnp.repeat(skip_gain, head_width).reshape(width // LANES, LANES)
    gain = norm_gain.reshape(width // LANES, LANES)
    sds = jax.ShapeDtypeStruct
    pg_rows = pre_gain.reshape(model // LANES, LANES)
    consts = (pg_rows,) + projections + (out_proj, conv_value, conv_state, vbias, sbias)
    consts += (head_pair, skip, gain)
    normed, gate_raw, vs_raw, z_raw, grad_normed_out, y, act, pre, stat, sin = pl.pallas_call(
        lead_kernel,
        grid=(tokens // lead,),
        in_specs=[by_rows(model), by_rows(model), by_chunks(16, T)]
        + [held(v) for v in consts],
        out_specs=[by_rows(c) for c in (model, width, wide, LANES, width, width, wide, wide)]
        + [by_chunks(2, T), by_chunks(N, width)],
        out_shape=[
            sds((tokens, model), bf16), sds((tokens, width), bf16), sds((tokens, wide), bf16),
            sds((tokens, LANES), f32), sds((tokens, width), bf16), sds((tokens, width), f32),
            sds((tokens, wide), bf16), sds((tokens, wide), bf16), sds((chunks, 2, T), f32),
            sds((chunks, N, width), bf16),
        ],
        scratch_shapes=[
            pltpu.VMEM((lead + 8, wide), f32), pltpu.VMEM((N, width), f32),
            pltpu.VMEM((lead // T, 3 * T, width), f32), pltpu.VMEM((lead // T, 2, T, LANES), f32),
            pltpu.VMEM((8, LANES), f32), pltpu.VMEM((LANES, width), bf16),
        ],
        name="lead",
    )(tokens_in, grad_out, aux, *consts)

    if n_tensor == 4:
        others = [swap(stat, "tensor", n_tensor, bit) for bit in (1, 2, 3)]
        stat = (stat + others[0]) + (others[1] + others[2])
    else:
        stat = butterfly(stat, "tensor", n_tensor)
    scale = lax.rsqrt(stat[:, 0] / inner_width + eps_value)
    slope_scale = scale * scale * scale * stat[:, 1] / inner_width
    scales = jnp.stack([scale, slope_scale], axis=1)
    steps = tokens // block
    upper = lax.axis_index("tensor") % 2 if n_tensor == 4 else 0
    upper = jnp.reshape(jnp.asarray(upper, jnp.int32), (1,))
    turn = lambda i, u: jnp.where(i < 2, 2 * i + 1 - u[0], 2 * i - 4 + u[0])
    turned = lambda columns: pl.BlockSpec((block, columns), lambda i, u: (turn(i, u), 0))
    kept_spec = lambda columns: pl.BlockSpec(
        (block, columns), lambda i, u: (jnp.maximum(i - steps // 2, 0), 0)
    )
    sent_spec = lambda columns: pl.BlockSpec(
        (block, columns), lambda i, u: (jnp.minimum(i, steps // 2 - 1), 0)
    )
    fixed = lambda rows, columns: pl.BlockSpec((rows, columns), lambda i, u: (0, 0))
    still = lambda value: pl.BlockSpec(
        value.shape, lambda i, u: (0,) * value.ndim, pipeline_mode=pl.Buffered(1)
    )
    halves = [sds((tokens // 2, model), bf16)] * 2
    gate_bf, mix, normed_out, sent, kept, gate_sums = pl.pallas_call(
        middle_kernel,
        grid_spec=pltpu.PrefetchScalarGridSpec(
            num_scalar_prefetch=1,
            grid=(steps,),
            in_specs=[turned(width)] * 4
            + [pl.BlockSpec((block // T, 2, T), lambda i, u: (turn(i, u), 0, 0))]
            + [still(skip), still(gain), still(out_proj)],
            out_specs=[turned(width)] * 3
            + [sent_spec(model), kept_spec(model), fixed(16, width)],
        ),
        out_shape=[sds((tokens, width), bf16)] * 3 + halves + [sds((16, width), f32)],
        name="middle",
    )(upper, gate_raw, grad_normed_out, y, act, scales, skip, gain, out_proj)
    grad_out_proj = dot_tn(normed_out, grad_out).astype(bf16)
    grad_gate_proj = dot_tn(normed, gate_bf).astype(bf16)
    grad_out_proj = lax.psum(grad_out_proj, "dp")
    grad_out_proj = grad_out_proj.astype(f32)
    grad_gate_proj = reduce_rows(grad_gate_proj, "dp", n_dp, f32)

    start = lax.axis_index("tensor") * (tokens // n_tensor)
    own = lambda v: lax.dynamic_slice_in_dim(v, start, tokens // n_tensor, 0)
    if n_tensor == 4:
        block_out = sum_quarters(kept, sent, (tokens_in,), (), block_kernel)
        block_out = gather_rows(block_out, "tensor", n_tensor, bf16, mixed=True)
    else:
        branch = scatter_halves(kept, sent, "tensor", n_tensor)
        block_out = (own(tokens_in).astype(f32) + branch).astype(bf16)
        block_out = lax.all_gather(block_out, "tensor", axis=0, tiled=True)

    consts = (conv_value, conv_state, head_pair, skip)
    given = (mix, y, act, pre, vs_raw, z_raw, sin, aux)
    out = [sds((tokens, full), bf16), sds((8 * (K + 2), wide), f32)]

    def of(value):
        row = lambda i, j: i * per_seq + per_seq - 1 - j
        if len(value.shape) == 2:
            return pl.BlockSpec((T, value.shape[1]), lambda i, j: (row(i, j), 0))
        return pl.BlockSpec((1,) + value.shape[1:], lambda i, j: (row(i, j), 0, 0))

    def whole(value):
        return pl.BlockSpec(value.shape, lambda i, j: (0, 0), pipeline_mode=pl.Buffered(1))

    packed, csum = pl.pallas_call(
        backward_kernel,
        grid=(seqs, per_seq),
        in_specs=[of(v) for v in given] + [whole(v) for v in consts],
        out_specs=[of(out[0]), pl.BlockSpec(out[1].shape, lambda i, j: (0, 0))],
        out_shape=out,
        scratch_shapes=[
            pltpu.VMEM((N, width), f32), pltpu.VMEM((T + 8, wide), f32),
            pltpu.VMEM((3 * T, width), f32), pltpu.VMEM((T, width), bf16),
            pltpu.VMEM((T, width), bf16), pltpu.VMEM((8, LANES), f32),
            pltpu.VMEM((8, LANES), f32), pltpu.VMEM((5, T, width), bf16),
            pltpu.VMEM((LANES, width), bf16), pltpu.VMEM((width, LANES), bf16),
        ],
        name="ssd_backward",
    )(*given, *consts)

    grad_packed = dot_tn(normed, packed).astype(bf16)
    grad_value_proj = grad_packed[:, :width]
    grad_state_proj = grad_packed[:, width:wide]
    grad_step_proj = grad_packed[:, wide : wide + heads].T
    sent, kept, gain_part = pl.pallas_call(
        group_kernel,
        grid_spec=pltpu.PrefetchScalarGridSpec(
            num_scalar_prefetch=1,
            grid=(steps,),
            in_specs=[turned(width), turned(full), turned(model)]
            + [still(w) for w in projections],
            out_specs=[sent_spec(model), kept_spec(model), fixed(8, model)],
            scratch_shapes=[pltpu.VMEM((block, model), bf16)],
        ),
        out_shape=halves + [sds((8, model), f32)],
        name="group_in",
    )(upper, gate_bf, packed, normed, *projections)
    gate_sums = jnp.pad(gate_sums, ((0, 0), (0, 2 * N)))
    sums = jnp.sum(jnp.concatenate([csum, gate_sums]).reshape(K + 4, 8, wide), axis=1)
    gain_part = jnp.sum(gain_part, axis=0) / pre_gain

    grad_value_proj = reduce_rows(grad_value_proj, "dp", n_dp, f32)

    if n_tensor == 4:
        gain_row = pre_gain[None, :]
        grad_in = sum_quarters(kept, sent, (tokens_in, grad_out), (gain_row,), input_kernel)
    else:
        grad_normed = scatter_halves(kept, sent, "tensor", n_tensor)
        own_hidden = own(tokens_in).astype(f32)
        own_inv = lax.rsqrt(jnp.mean(own_hidden * own_hidden, axis=1, keepdims=True) + eps_value)
        weighted = pre_gain * grad_normed
        grad_hidden = own_inv * weighted - own_hidden * (own_inv * own_inv * own_inv) * jnp.mean(
            weighted * own_hidden, axis=1, keepdims=True
        )
        grad_in = (own(grad_out).astype(f32) + grad_hidden).astype(bf16)
    grad_in = lax.all_gather(grad_in, "tensor", axis=0, tiled=True)
    grad_in = copy_rows(grad_in)

    gain_rows = model // (2 * N)
    extra = jnp.concatenate([sums[:, width:], gain_part.reshape(gain_rows, 2 * N)], axis=0)
    unit = n_tensor * math.lcm(16, model // math.gcd(model, 2 * N))
    gap = -(model + extra.shape[0]) % unit
    extra = jnp.pad(extra, ((0, gap), (0, 0))).astype(bf16)
    shared = jnp.concatenate([grad_state_proj, extra], axis=0)
    shared = scatter_sum(shared, "tensor", n_tensor).astype(bf16)
    small = jnp.concatenate([jnp.pad(sums, ((0, 0), (0, model - wide))), grad_step_proj], axis=0)
    part = shared.shape[0]
    flat = part * 2 * N // model
    both = jnp.concatenate([shared.reshape(flat, model), small.astype(bf16)], axis=0)
    both = butterfly(both, "dp", n_dp)
    shared, small = both[:flat].reshape(part, 2 * N), both[flat:].astype(f32)
    shared = gather_rows(shared, "tensor", n_tensor, bf16)
    grad_state_proj = shared[:model].astype(f32)
    state_sums = shared[model : model + K + 4].astype(f32)
    grad_pre_gain = shared[model + K + 4 : model + K + 4 + gain_rows].reshape(model).astype(f32)
    sums = small[: K + 4]
    grad_step_proj = small[K + 4 :].T
    grad_skip = jnp.sum(sums[K + 3, :width].reshape(heads, head_width), axis=1)
    return (
        block_out,
        grad_in,
        grad_pre_gain,
        grad_gate_proj,
        grad_value_proj,
        grad_state_proj,
        grad_step_proj,
        sums[:K, :width],
        sums[K, :width],
        state_sums[:K],
        state_sums[K],
        sums[K + 1, :heads],
        sums[K + 1, LANES : LANES + heads] * decay_rate,
        grad_skip,
        sums[K + 2, :width],
        grad_out_proj,
    )


def solution(mesh):
    t = P("tensor")
    cols = P(None, "tensor")
    in_specs = (
        P("dp", None), P("dp"), P(), cols, cols, P(), cols, cols, t, P(), P(), t, t, t, t,
        P("tensor", None), P("dp", None),
    )
    out_specs = (
        P("dp", None), P("dp", None), P(), cols, cols, P(), cols, cols, t, P(), P(), t, t, t, t,
        P("tensor", None),
    )
    n_dp, n_tensor = mesh.shape["dp"], mesh.shape["tensor"]

    def body(*args):
        return on_device(*args, n_dp=n_dp, n_tensor=n_tensor)

    return jax.shard_map(body, mesh=mesh, in_specs=in_specs, out_specs=out_specs, check_vma=False)
```

```python
import math

import jax
import jax.numpy as jnp
from jax import lax
from jax.experimental import pallas as pl
from jax.experimental.pallas import tpu as pltpu
from jax.sharding import PartitionSpec as P


N = 128
K = 4
SEQ_LEN = 1024
T = 128
LANES = 128
HALF = 64
NEG = -1e30
eps_value = 1e-05
f32 = jnp.float32
bf16 = jnp.bfloat16


def dot(a, b):
    return jnp.dot(a, b, preferred_element_type=f32)


def dot_nt(a, b):
    return lax.dot_general(a, b, (((1,), (1,)), ((), ())), preferred_element_type=f32)


def dot_tn(a, b):
    return lax.dot_general(a, b, (((0,), (0,)), ((), ())), preferred_element_type=f32)


def sigmoid(v):
    return 0.5 * jnp.tanh(0.5 * v) + 0.5


def two_terms(v):
    high = v.astype(bf16)
    return high, (v - high.astype(f32)).astype(bf16)


def paired(v):
    high, low = two_terms(v)
    lane = lax.broadcasted_iota(jnp.int32, v.shape, 1)
    return jnp.where(lane < HALF, high, low)


def sum_rows(v):
    total = v[0:8]
    for row in range(8, v.shape[0], 8):
        total = total + v[row : row + 8]
    return total


def head_rows(heads_ref, lane_ref):
    count = heads_ref.shape[1]
    lane_ref[...] = jnp.zeros_like(lane_ref)
    lane_ref[0:2, 0:count] = heads_ref[...]
    lane_ref[0:2, HALF : HALF + count] = heads_ref[...]
    return lane_ref[0:1, :], -jnp.exp(lane_ref[1:2, :])


def ones_where(condition):
    return jnp.where(condition, 1.0, 0.0).astype(bf16)


def expansion(shape, head_width):
    lane = lax.broadcasted_iota(jnp.int32, shape, 0)
    owner = lax.broadcasted_iota(jnp.int32, shape, 1) // head_width
    return ones_where((lane == owner) | (lane == owner + HALF))


def reduction(shape, head_width):
    owner = lax.broadcasted_iota(jnp.int32, shape, 0) // head_width
    return ones_where(lax.broadcasted_iota(jnp.int32, shape, 1) == owner)


def triangle():
    row = lax.broadcasted_iota(jnp.int32, (T, T), 0)
    col = lax.broadcasted_iota(jnp.int32, (T, T), 1)
    return row, col


def head_terms(z_ref, bias, rate, aux, tri, e_ref, ex_ref):
    z = z_ref[...] + bias
    tail = jnp.exp(-jnp.abs(z))
    step = jnp.maximum(z, 0.0) + jnp.log1p(tail)
    high, low = two_terms(step * rate)
    cum = dot(tri, high) + dot(tri, low)
    end = cum[T - 1 : T]
    dst = jnp.exp(cum) * aux[:, 3:4]
    dend = jnp.exp(end - cum) * aux[:, 4:5]
    total = jnp.exp(jnp.broadcast_to(end, (8, LANES))) * aux[T - 1 : T, 3:4]
    stacked = jnp.concatenate([paired(step), paired(dend), paired(dst)], axis=0)
    ex_ref[...] = dot(stacked, e_ref[...])
    carry = dot(paired(total), e_ref[...])[0:1]
    return z, step, cum, cum.T, carry


def taps_of(c, width, vtaps_ref, staps_ref):
    ref, at = (vtaps_ref, c) if c.start < width else (staps_ref, slice(c.start - width, c.stop - width))
    return lambda s: ref[K - 1 - s : K - s, at]


def lead_kernel(
    tokens_ref, go_ref, aux_ref, pg_ref, gate_w, value_w, state_w, step_w, out_w,
    vtaps_ref, staps_ref, vbias_ref, sbias_ref, heads_ref, skip_ref, ng_ref,
    normed_ref, gate_ref, vs_ref, z_ref, gno_ref, y_ref, act_ref, pre_ref, stat_ref, sin_ref,
    ext_ref, state_ref, ex_ref, sum_ref, lane_ref, e_ref,
):
    rows, width = gate_ref.shape
    chunks = range(rows // T)

    @pl.when(pl.program_id(0) == 0)
    def _():
        e_ref[...] = expansion(e_ref.shape, width // heads_ref.shape[1])

    @pl.when(pl.program_id(0) % (SEQ_LEN // rows) == 0)
    def _():
        state_ref[...] = jnp.zeros_like(state_ref)
        ext_ref[0:8, :] = jnp.zeros_like(ext_ref[0:8, :])

    part = 32
    for lo in range(0, rows, part):
        r = slice(lo, lo + part)
        hidden = tokens_ref[r, :].astype(f32)
        inv = lax.rsqrt(jnp.mean(hidden * hidden, axis=1, keepdims=True) + eps_value)
        for k in range(pg_ref.shape[0]):
            c = slice(k * LANES, (k + 1) * LANES)
            normed_ref[r, c] = (hidden[:, c] * inv * pg_ref[k : k + 1, :]).astype(bf16)
    z = dot_nt(normed_ref[...], step_w[...])
    z_ref[...] = jnp.zeros_like(z_ref)
    z_ref[:, : z.shape[1]] = z
    z_ref[:, HALF : HALF + z.shape[1]] = z
    raw = dot(normed_ref[...], state_w[...])
    ext_ref[8:, width:] = raw
    vs_ref[:, width:] = raw.astype(bf16)
    at = [pl.ds(k * T, T) for k in chunks]
    bias, rate = head_rows(heads_ref, lane_ref)
    row, col = triangle()
    tri = ones_where(row >= col)
    aux = [aux_ref[k].T for k in chunks]
    terms = [
        head_terms(z_ref.at[at[k]], bias, rate, aux[k], tri, e_ref, ex_ref.at[k])
        for k in chunks
    ]
    keep = [
        [jnp.broadcast_to(aux[k][:, s : s + 1], (T, LANES)) for s in range(K - 1)] for k in chunks
    ]

    def activate(c, k):
        lo = 8 + k * T
        tap, shift = taps_of(c, width, vtaps_ref, staps_ref), c.start // LANES
        if c.start < width:
            pre = vbias_ref[shift : shift + 1, :]
        else:
            pre = sbias_ref[shift - width // LANES : shift - width // LANES + 1, :]
        pre = pre + tap(0) * ext_ref[lo : lo + T, c]
        for s in range(1, K):
            pre = pre + tap(s) * (ext_ref[lo - s : lo - s + T, c] * keep[k][s - 1])
        half = 0.5 * pre
        act = half + half * jnp.tanh(half)
        act_bf = act.astype(bf16)
        pre_ref[at[k], c] = pre.astype(bf16)
        act_ref[at[k], c] = act_bf
        return act, act_bf

    b_flip, c_mats, scores, fades = [], [], [], []
    for k in chunks:
        _, b_mat = activate(slice(width, width + N), k)
        _, c_mat = activate(slice(width + N, width + 2 * N), k)
        b_flip.append(b_mat.T)
        c_mats.append(c_mat)
        scores.append(dot_nt(c_mat, b_mat))
        same = (aux[k][:, 5:6] == aux_ref[k, 5:6, :]) & (row >= col)
        fades.append(jnp.where(same, 0.0, NEG))
    first = lax.broadcasted_iota(jnp.int32, (T, LANES), 1) < HALF
    sum_ref[...] = jnp.zeros_like(sum_ref)
    span = 2 * LANES if width % (2 * LANES) == 0 else LANES
    for lo in range(0, width, span):
        group = slice(lo, lo + span)
        raw = dot(normed_ref[...], value_w[:, group])
        ext_ref[8:, group] = raw
        vs_ref[:, group] = raw.astype(bf16)
        gates = dot(normed_ref[...], gate_w[:, group])
        gate_ref[:, group] = gates.astype(bf16)
        gnos = dot_nt(go_ref[...], out_w[group, :])
        gno_ref[:, group] = gnos.astype(bf16)
        for pair in range(lo // LANES, (lo + span) // LANES):
            c = slice(pair * LANES, (pair + 1) * LANES)
            inside = slice(pair * LANES - lo, (pair + 1) * LANES - lo)
            for k in chunks:
                _, _, cum, cum_t, carry = terms[k]
                r = slice(k * T, (k + 1) * T)
                act, act_bf = activate(c, k)
                xt_full = act_bf.astype(f32) * ex_ref[k, 0:T, c]
                xt = xt_full.astype(bf16)
                xd = (xt_full * ex_ref[k, T : 2 * T, c]).astype(bf16)
                mixes = []
                for h in (2 * pair, 2 * pair + 1):
                    decay = jnp.exp(fades[k] + (cum[:, h : h + 1] - cum_t[h : h + 1, :]))
                    mixes.append((scores[k] * decay).astype(bf16))
                zero = jnp.zeros_like(xt)
                blocks = [jnp.where(first, xt, zero), jnp.where(first, zero, xt)]
                state = state_ref[:, c]
                state_bf = state.astype(bf16)
                sin_ref[k, :, c] = state_bf
                y = dot(jnp.concatenate(mixes, axis=1), jnp.concatenate(blocks, axis=0))
                y = y + ex_ref[k, 2 * T : 3 * T, c] * dot(c_mats[k], state_bf)
                y_ref[r, c] = y
                state_ref[:, c] = state * carry[:, c] + dot(b_flip[k], xd)
                half = 0.5 * gates[r, inside]
                gated = (y + skip_ref[pair : pair + 1, :] * act) * (half + half * jnp.tanh(half))
                sum_ref[k, 0] += gated * gated
                sum_ref[k, 1] += gated * ng_ref[pair : pair + 1, :] * gnos[r, inside]
    for k in chunks:
        for s in range(2):
            stat_ref[k, s : s + 1, :] = jnp.sum(sum_ref[k, s].T, axis=0, keepdims=True)
    ext_ref[0:8, :] = ext_ref[rows : rows + 8, :]


def store_half(value, sent_ref, kept_ref):
    first = pl.program_id(0) < pl.num_programs(0) // 2

    @pl.when(first)
    def _():
        sent_ref[...] = value

    @pl.when(jnp.logical_not(first))
    def _():
        kept_ref[...] = value


def middle_kernel(
    _, gate_ref, gno_ref, y_ref, act_ref, stat_ref, skip_ref, ng_ref, out_w,
    gate_grad_ref, mix_ref, normed_ref, sent_ref, kept_ref, csum_ref,
):
    @pl.when(pl.program_id(0) == 0)
    def _():
        csum_ref[...] = jnp.zeros_like(csum_ref)

    def one(chunk, carry):
        r = pl.ds(pl.multiple_of(chunk * T, T), T)
        scale = jnp.broadcast_to(stat_ref[chunk, 0:1, :], (LANES, T)).T
        slope_scale = jnp.broadcast_to(stat_ref[chunk, 1:2, :], (LANES, T)).T
        for pair in range(gate_ref.shape[1] // LANES):
            c = slice(pair * LANES, (pair + 1) * LANES)
            gate = gate_ref[r, c].astype(f32)
            logistic = sigmoid(gate)
            swish = gate * logistic
            x = act_ref[r, c].astype(f32)
            gno = gno_ref[r, c].astype(f32)
            ssd = y_ref[r, c] + skip_ref[pair : pair + 1, :] * x
            gated = ssd * swish
            unit = gated * scale
            normed_ref[r, c] = (unit * ng_ref[pair : pair + 1, :]).astype(bf16)
            grad_gated = scale * (gno * ng_ref[pair : pair + 1, :]) - slope_scale * gated
            csum_ref[0:8, c] += sum_rows(gno * unit)
            grad_mix = grad_gated * swish
            grad_gate = grad_gated * ssd * (logistic + swish * (1.0 - logistic))
            gate_grad_ref[r, c] = grad_gate.astype(bf16)
            csum_ref[8:16, c] += sum_rows(grad_mix * x)
            mix_ref[r, c] = grad_mix.astype(bf16)
        return carry

    lax.fori_loop(0, stat_ref.shape[0], one, 0)
    store_half(dot(normed_ref[...], out_w[...]).astype(bf16), sent_ref, kept_ref)


def backward_kernel(
    mix_ref, y_ref, act_ref, pre_ref, vs_ref, z_ref, sin_ref, aux_ref,
    vtaps_ref, staps_ref, heads_ref, skip_ref,
    grad_ref, csum_ref,
    back_ref, ext_ref, ex_ref, xd_ref, gd_ref, through_ref, lane_ref, part_ref, e_ref, er_ref,
):
    width = mix_ref.shape[1]

    @pl.when((pl.program_id(0) == 0) & (pl.program_id(1) == 0))
    def _():
        csum_ref[...] = jnp.zeros_like(csum_ref)
        e_ref[...] = expansion(e_ref.shape, width // heads_ref.shape[1])
        er_ref[...] = reduction(er_ref.shape, width // heads_ref.shape[1])

    @pl.when(pl.program_id(1) == 0)
    def _():
        back_ref[...] = jnp.zeros_like(back_ref)
        ext_ref[T : T + 8, :] = jnp.zeros_like(ext_ref[T : T + 8, :])

    row, col = triangle()
    tri, triu = ones_where(row >= col), ones_where(row <= col)
    bias, rate = head_rows(heads_ref, lane_ref)
    aux = aux_ref[0].T
    z, step, cum, cum_t, carry = head_terms(z_ref, bias, rate, aux, tri, e_ref, ex_ref)
    keep = [jnp.broadcast_to(aux[:, 5 + s : 6 + s], (T, LANES)) for s in range(1, K)]
    b_mat = act_ref[:, width : width + N]
    c_mat = act_ref[:, width + N : width + 2 * N]
    scores_t = dot_nt(b_mat, c_mat)
    same = (aux[:, 5:6] == aux_ref[0, 5:6, :]) & (row <= col)
    fade = jnp.where(same, 0.0, NEG)
    lane = lax.broadcasted_iota(jnp.int32, (T, LANES), 1)
    first = lane < HALF
    back_bf = back_ref[...].astype(bf16)

    def conv_back(grad_pre, c):
        ext_ref[0:T, c] = grad_pre
        raw = vs_ref[:, c].astype(f32)
        tap = taps_of(c, width, vtaps_ref, staps_ref)
        grad_raw = tap(0) * grad_pre
        csum_ref[8 * (K - 1) : 8 * K, c] += sum_rows(grad_pre * raw)
        csum_ref[8 * K : 8 * K + 8, c] += sum_rows(grad_pre)
        for s in range(1, K):
            moved = ext_ref[s : s + T, c] * keep[s - 1]
            grad_raw = grad_raw + tap(s) * moved
            csum_ref[8 * (K - 1 - s) : 8 * (K - s), c] += sum_rows(moved * raw)
        return grad_raw

    def slope(c):
        pre = pre_ref[:, c].astype(f32)
        logistic = sigmoid(pre)
        return logistic * (1.0 + pre * (1.0 - logistic))

    def through_of(value):
        high, low = two_terms(sum_rows(value))
        through = dot(high, er_ref[...]) + dot(low, er_ref[...])
        return jnp.broadcast_to(jnp.sum(through, axis=0, keepdims=True), (8, LANES))

    grad_scores = jnp.zeros((T, T), f32)
    through_ref[...] = through_of(sin_ref[0].astype(f32) * back_ref[...] * carry)
    for pair in range(width // LANES):
        c = slice(pair * LANES, (pair + 1) * LANES)
        x = act_ref[:, c].astype(f32)
        y = y_ref[:, c]
        g = mix_ref[:, c]
        grad_mix = g.astype(f32)
        step_x = ex_ref[0:T, c]
        dend_x = ex_ref[T : 2 * T, c]
        gd_ref[:, c] = (grad_mix * ex_ref[2 * T : 3 * T, c]).astype(bf16)
        xt_full = x * step_x
        xt = xt_full.astype(bf16)
        xd_ref[:, c] = (xt_full * dend_x).astype(bf16)
        zero = jnp.zeros_like(g)
        g_blocks = jnp.concatenate([jnp.where(first, g, zero), jnp.where(first, zero, g)], axis=0)
        x_blocks = jnp.concatenate([jnp.where(first, xt, zero), jnp.where(first, zero, xt)], axis=0)
        products = dot_nt(x_blocks, g)
        mixes = []
        for k, h in enumerate((2 * pair, 2 * pair + 1)):
            decay = jnp.exp(fade + (cum_t[h : h + 1, :] - cum[:, h : h + 1]))
            mixes.append((scores_t * decay).astype(bf16))
            grad_scores = grad_scores + products[k * T : (k + 1) * T] * decay
        u_in = dot(jnp.concatenate(mixes, axis=1), g_blocks)
        u_far = dend_x * dot(b_mat, back_bf[:, c])
        u = u_in + u_far
        y_far = ex_ref[2 * T : 3 * T, c] * dot(c_mat, sin_ref[0, :, c])
        xt_wide = xt.astype(f32)
        part_ref[0, :, c], part_ref[1, :, c] = two_terms(grad_mix * (y - y_far) - xt_wide * u_in)
        part_ref[2, :, c] = (grad_mix * y_far).astype(bf16)
        part_ref[3, :, c] = (xt_wide * u_far).astype(bf16)
        part_ref[4, :, c] = (x * u).astype(bf16)
        grad_value = step_x * u + skip_ref[pair : pair + 1, :] * grad_mix
        grad_ref[:, c] = conv_back(grad_value * slope(c), c).astype(bf16)

    gs_bf = grad_scores.astype(bf16)
    grad_b = dot(gs_bf, c_mat) + dot_nt(xd_ref[...], back_bf)
    grad_c = dot_tn(gs_bf, b_mat) + dot_nt(gd_ref[...], sin_ref[0])
    for k, grad in enumerate((grad_b, grad_c)):
        c = slice(width + k * N, width + (k + 1) * N)
        grad_ref[:, c] = conv_back(grad * slope(c), c).astype(bf16)
    ext_ref[T : T + 8, :] = ext_ref[0:8, :]

    by_head = [dot(part_ref[k], er_ref[...]) for k in range(5)]
    col_far, direct = by_head[3:]
    high, low = two_terms(by_head[0] + by_head[1] + by_head[2])
    grad_acc = through_ref[0:1, :] + (dot(triu, high) + dot(triu, low))
    high, low = two_terms(col_far)
    grad_acc = grad_acc + (dot(tri, high) + dot(tri, low)) - col_far
    grad_step = direct + grad_acc * rate
    grad_z = grad_step * sigmoid(z)
    csum_ref[8 * (K + 1) : 8 * (K + 2), 0:LANES] += sum_rows(grad_z)
    csum_ref[8 * (K + 1) : 8 * (K + 2), LANES : 2 * LANES] += sum_rows(grad_acc * step)
    grad_ref[:, width + 2 * N :] = grad_z.astype(bf16)

    new_back = back_ref[...] * carry + dot_tn(c_mat, gd_ref[...])
    back_ref[...] = new_back


def bits_of(size):
    return [1 << k for k in range(size.bit_length() - 1)] if size & (size - 1) == 0 else None


def swap(value, axis, size, bit):
    return lax.ppermute(value, axis, [(i, i ^ bit) for i in range(size)])


def block_of(rows):
    return max(b for b in range(16, 513, 16) if rows % b == 0)


def place(buffer, value, slot, dtype, parts):
    rows, width = value.shape
    block = block_of(rows)
    count = rows // block

    def kernel(slot_ref, value_ref, *refs):
        refs[-1][...] = value_ref[...].astype(dtype)

    out = jax.ShapeDtypeStruct((parts * rows, width), dtype)
    given = () if buffer is None else (buffer,)
    return pl.pallas_call(
        kernel,
        grid_spec=pltpu.PrefetchScalarGridSpec(
            num_scalar_prefetch=1,
            grid=(count,),
            in_specs=[pl.BlockSpec((block, width), lambda i, s: (i, 0))]
            + [pl.BlockSpec(memory_space=pl.ANY) for _ in given],
            out_specs=pl.BlockSpec((block, width), lambda i, s: (s[0] * count + i, 0)),
        ),
        out_shape=out,
        input_output_aliases={2: 0} if given else {},
        name="place",
    )(jnp.reshape(slot, (1,)).astype(jnp.int32), value, *given)


def copy_rows(value):
    def kernel(value_ref, out_ref):
        out_ref[...] = value_ref[...]

    spec = pl.BlockSpec((block_of(value.shape[0]), value.shape[1]), lambda i: (i, 0))
    return pl.pallas_call(
        kernel,
        grid=(value.shape[0] // spec.block_shape[0],),
        in_specs=[spec],
        out_specs=spec,
        out_shape=jax.ShapeDtypeStruct(value.shape, value.dtype),
        name="copy_rows",
    )(value)


def assemble(pieces, slots, dtype):
    rows, width = pieces[0].shape

    def kernel(slots_ref, *refs):
        for k, ref in enumerate(refs[:-1]):

            @pl.when(pl.program_id(0) == k)
            def _(ref=ref):
                refs[-1][...] = ref[...].astype(dtype)

    return pl.pallas_call(
        kernel,
        grid_spec=pltpu.PrefetchScalarGridSpec(
            num_scalar_prefetch=1,
            grid=(len(pieces),),
            in_specs=[pl.BlockSpec((rows, width), lambda i, s: (0, 0)) for _ in pieces],
            out_specs=pl.BlockSpec((rows, width), lambda i, s: (s[i], 0)),
        ),
        out_shape=jax.ShapeDtypeStruct((len(pieces) * rows, width), dtype),
        name="assemble",
    )(jnp.stack(slots).astype(jnp.int32), *pieces)


def join(value, other, upper):
    rows, width = value.shape
    block = block_of(rows)
    count = rows // block

    def kernel(upper_ref, value_ref, other_ref, out_ref):
        mine = pl.program_id(0) == upper_ref[0]

        @pl.when(mine)
        def _():
            out_ref[...] = value_ref[...]

        @pl.when(jnp.logical_not(mine))
        def _():
            out_ref[...] = other_ref[...]

    return pl.pallas_call(
        kernel,
        grid_spec=pltpu.PrefetchScalarGridSpec(
            num_scalar_prefetch=1,
            grid=(2, count),
            in_specs=[
                pl.BlockSpec((block, width), lambda h, i, u: (jnp.where(h == u[0], i, 0), 0)),
                pl.BlockSpec((block, width), lambda h, i, u: (jnp.where(h == u[0], 0, i), 0)),
            ],
            out_specs=pl.BlockSpec((block, width), lambda h, i, u: (h * count + i, 0)),
        ),
        out_shape=jax.ShapeDtypeStruct((2 * rows, width), value.dtype),
        name="join",
    )(jnp.reshape(upper, (1,)).astype(jnp.int32), value, other)


def add_parts(parts, start, rows):
    total = None
    for value, base in parts:
        piece = lax.dynamic_slice_in_dim(value, base + start, rows, 0).astype(f32)
        total = piece if total is None else total + piece
    return total


def sum_quarters(kept, sent, arrays, rows, kernel):
    index = lax.axis_index("tensor")
    other = swap(sent, "tensor", 4, 1)
    upper = index // 2
    quarter, width = kept.shape[0] // 2, kept.shape[1]
    out = add_parts([(kept, 0), (other, 0)], (1 - upper) * quarter, quarter).astype(kept.dtype)
    last = swap(out, "tensor", 4, 2)
    block = 2 * T if quarter % (2 * T) == 0 else T
    count = quarter // block
    half = pl.BlockSpec((block, width), lambda i, s: (s[1] * count + i, 0))
    own = pl.BlockSpec((block, width), lambda i, s: (s[0] * count + i, 0))
    plain = pl.BlockSpec((block, width), lambda i, s: (i, 0))
    return pl.pallas_call(
        kernel,
        grid_spec=pltpu.PrefetchScalarGridSpec(
            num_scalar_prefetch=1,
            grid=(count,),
            in_specs=[half, half, plain]
            + [own for _ in arrays]
            + [pl.BlockSpec(v.shape, lambda i, s: (0, 0)) for v in rows],
            out_specs=plain,
        ),
        out_shape=jax.ShapeDtypeStruct((quarter, width), bf16),
        name="quarter",
    )(jnp.stack([index, upper]).astype(jnp.int32), kept, other, last, *arrays, *rows)


def block_kernel(_, kept_ref, other_ref, last_ref, tokens_ref, out_ref):
    total = kept_ref[...].astype(f32) + other_ref[...].astype(f32) + last_ref[...].astype(f32)
    out_ref[...] = (tokens_ref[...].astype(f32) + total).astype(bf16)


def input_kernel(_, kept_ref, other_ref, last_ref, tokens_ref, grad_ref, gain_ref, out_ref):
    part = 64

    def one(index, carry):
        r = pl.ds(pl.multiple_of(index * part, part), part)
        total = kept_ref[r, :].astype(f32) + other_ref[r, :].astype(f32) + last_ref[r, :].astype(f32)
        hidden = tokens_ref[r, :].astype(f32)
        inv = lax.rsqrt(jnp.mean(hidden * hidden, axis=1, keepdims=True) + eps_value)
        weighted = gain_ref[0:1, :] * total
        mean = jnp.mean(weighted * hidden, axis=1, keepdims=True)
        grad_hidden = inv * weighted - hidden * (inv * inv * inv * mean)
        out_ref[r, :] = (grad_ref[r, :].astype(f32) + grad_hidden).astype(bf16)
        return carry

    lax.fori_loop(0, out_ref.shape[0] // part, one, 0)


def scatter_halves(kept, sent, axis, size):
    bits = bits_of(size)
    if size != 4:
        quarter = (2, kept.shape[0] // 2, kept.shape[1])
        value = jnp.stack([kept.reshape(quarter), sent.reshape(quarter)], axis=1)
        value = value.reshape(2 * kept.shape[0], kept.shape[1])
        return lax.psum_scatter(value, axis, scatter_dimension=0, tiled=True).astype(f32)
    other = swap(sent, axis, size, bits[0])
    return scatter_parts([(kept, 0), (other, 0)], axis, size, bits[1:])


def scatter_sum(value, axis, size):
    bits = bits_of(size)
    if bits is None:
        return lax.psum_scatter(value, axis, scatter_dimension=0, tiled=True).astype(f32)
    return scatter_parts([(value, 0)], axis, size, bits)


def scatter_parts(parts, axis, size, bits):
    index = lax.axis_index(axis)
    value = parts[0][0]
    rows = value.shape[0]
    for bit in bits:
        upper = (index // bit) % 2
        rows = rows // 2
        sent = add_parts(parts, (1 - upper) * rows, rows).astype(value.dtype)
        other = swap(sent, axis, size, bit)
        parts = [(part, base + upper * rows) for part, base in parts] + [(other, 0)]
    return add_parts(parts, 0, rows)


def rows_are_few(value):
    return value.size * value.dtype.itemsize < 2**18


def gather_rows(value, axis, size, dtype, mixed=False):
    index = lax.axis_index(axis)
    bits = bits_of(size)
    if bits is None or len(bits) < 2:
        return lax.all_gather(value, axis, axis=0, tiled=True).astype(dtype)
    for bit in bits[:1:-1]:
        other = swap(value, axis, size, bit)
        value = join(value, other, (index // bit) % 2)
    outer, inner = bits[:2]
    near = swap(value, axis, size, inner)
    far = swap(value, axis, size, outer)
    both = swap(near, axis, size, outer)
    side, half = (index // outer) % 2, (index // inner) % 2

    def slot(flip_outer, flip_inner):
        x, y = (1 - side if flip_outer else side), (1 - half if flip_inner else half)
        return x + 2 * y if mixed else 2 * x + y

    if rows_are_few(value):
        pieces = (value, far, near, both)
        return assemble(pieces, [slot(0, 0), slot(1, 0), slot(0, 1), slot(1, 1)], dtype)
    buffer = None
    for piece, flips in ((value, (0, 0)), (far, (1, 0)), (near, (0, 1)), (both, (1, 1))):
        buffer = place(buffer, piece, slot(*flips), dtype, 4)
    return buffer


def reduce_rows(value, axis, size, dtype):
    part = scatter_sum(value, axis, size).astype(value.dtype)
    return gather_rows(part, axis, size, dtype)


def butterfly(value, axis, size):
    bits = bits_of(size)
    if bits is None:
        return lax.psum(value, axis)
    for bit in bits:
        value = value + swap(value, axis, size, bit)
    return value


def token_aux(segments):
    count = segments.shape[0]
    seg = segments.astype(f32)
    position = jnp.arange(count, dtype=jnp.int32) % SEQ_LEN
    columns = []
    lifted = []
    for s in range(1, K):
        before = jnp.concatenate([jnp.zeros((s,), f32), seg[:-s]])
        keep = ((position >= s) & (seg == before)).astype(f32)
        columns.append(keep)
        lifted.append(jnp.concatenate([keep[s:], jnp.zeros((s,), f32)]))
    chunked = seg.reshape(count // T, T)
    last = chunked[:, T - 1]
    starts = (jnp.arange(count // T, dtype=jnp.int32) * T) % SEQ_LEN == 0
    before = jnp.where(starts, -1.0, jnp.concatenate([jnp.zeros((1,), f32), last[:-1]]))
    columns.append((chunked == before[:, None]).astype(f32).reshape(count))
    columns.append((chunked == last[:, None]).astype(f32).reshape(count))
    columns.append(seg)
    rows = [row.reshape(count // T, T) for row in columns + lifted]
    return jnp.stack(rows + [rows[0]] * (16 - len(rows)), axis=1)


def group_kernel(
    _, gate_ref, packed_ref, normed_ref, gate_w, value_w, state_w, step_w,
    sent_ref, kept_ref, gain_ref, in_ref,
):
    weights = (value_w, state_w)
    steps = packed_ref[:, value_w.shape[1] + state_w.shape[1] :][:, : step_w.shape[0]]

    @pl.when(pl.program_id(0) == 0)
    def _():
        gain_ref[...] = jnp.zeros_like(gain_ref)

    model = in_ref.shape[1]
    part = model // 3 if model % 384 == 0 else model

    def one(index, carry):
        c = pl.ds(pl.multiple_of(index * part, part), part)
        total, at = dot_nt(gate_ref[...], gate_w[c, :]) + dot(steps, step_w[:, c]), 0
        for w in weights:
            total = total + dot_nt(packed_ref[:, at : at + w.shape[1]], w[c, :])
            at += w.shape[1]
        rounded = total.astype(bf16)
        in_ref[:, c] = rounded
        gain_ref[:, c] += sum_rows(rounded.astype(f32) * normed_ref[:, c].astype(f32))
        return carry

    lax.fori_loop(0, model // part, one, 0)
    store_half(in_ref[...], sent_ref, kept_ref)


def on_device(
    tokens_in, segments, pre_gain, gate_proj, value_proj, state_proj, step_proj, conv_value,
    conv_value_bias, conv_state, conv_state_bias, step_bias, decay_log, skip_gain, norm_gain,
    out_proj, grad_out, *, n_dp, n_tensor,
):
    tokens, model = tokens_in.shape
    width = gate_proj.shape[1]
    heads = step_proj.shape[1]
    head_width = width // heads
    chunks = tokens // T
    seqs = tokens // SEQ_LEN
    per_seq = SEQ_LEN // T
    wide = width + 2 * N
    full = wide + LANES
    inner_width = width * n_tensor

    aux = token_aux(segments)

    projections = (gate_proj, value_proj, state_proj, step_proj.T)
    block = tokens // 4
    lead = 2 * T
    by_rows = lambda columns: pl.BlockSpec((lead, columns), lambda i: (i, 0))
    by_chunks = lambda *shape: pl.BlockSpec((lead // T,) + shape, lambda i: (i, 0, 0))
    held = lambda value: pl.BlockSpec(
        value.shape, lambda i: (0,) * value.ndim, pipeline_mode=pl.Buffered(1)
    )
    vbias = conv_value_bias.reshape(width // LANES, LANES)
    sbias = conv_state_bias.reshape(2 * N // LANES, LANES)
    head_pair = jnp.stack([step_bias, decay_log])
    decay_rate = -jnp.exp(decay_log)
    skip = jnp.repeat(skip_gain, head_width).reshape(width // LANES, LANES)
    gain = norm_gain.reshape(width // LANES, LANES)
    sds = jax.ShapeDtypeStruct
    pg_rows = pre_gain.reshape(model // LANES, LANES)
    consts = (pg_rows,) + projections + (out_proj, conv_value, conv_state, vbias, sbias)
    consts += (head_pair, skip, gain)
    normed, gate_raw, vs_raw, z_raw, grad_normed_out, y, act, pre, stat, sin = pl.pallas_call(
        lead_kernel,
        grid=(tokens // lead,),
        in_specs=[by_rows(model), by_rows(model), by_chunks(16, T)]
        + [held(v) for v in consts],
        out_specs=[by_rows(c) for c in (model, width, wide, LANES, width, width, wide, wide)]
        + [by_chunks(2, T), by_chunks(N, width)],
        out_shape=[
            sds((tokens, model), bf16), sds((tokens, width), bf16), sds((tokens, wide), bf16),
            sds((tokens, LANES), f32), sds((tokens, width), bf16), sds((tokens, width), f32),
            sds((tokens, wide), bf16), sds((tokens, wide), bf16), sds((chunks, 2, T), f32),
            sds((chunks, N, width), bf16),
        ],
        scratch_shapes=[
            pltpu.VMEM((lead + 8, wide), f32), pltpu.VMEM((N, width), f32),
            pltpu.VMEM((lead // T, 3 * T, width), f32), pltpu.VMEM((lead // T, 2, T, LANES), f32),
            pltpu.VMEM((8, LANES), f32), pltpu.VMEM((LANES, width), bf16),
        ],
        name="lead",
    )(tokens_in, grad_out, aux, *consts)

    if n_tensor == 4:
        others = [swap(stat, "tensor", n_tensor, bit) for bit in (1, 2, 3)]
        stat = (stat + others[0]) + (others[1] + others[2])
    else:
        stat = butterfly(stat, "tensor", n_tensor)
    scale = lax.rsqrt(stat[:, 0] / inner_width + eps_value)
    slope_scale = scale * scale * scale * stat[:, 1] / inner_width
    scales = jnp.stack([scale, slope_scale], axis=1)
    steps = tokens // block
    upper = lax.axis_index("tensor") % 2 if n_tensor == 4 else 0
    upper = jnp.reshape(jnp.asarray(upper, jnp.int32), (1,))
    turn = lambda i, u: jnp.where(i < 2, 2 * i + 1 - u[0], 2 * i - 4 + u[0])
    turned = lambda columns: pl.BlockSpec((block, columns), lambda i, u: (turn(i, u), 0))
    kept_spec = lambda columns: pl.BlockSpec(
        (block, columns), lambda i, u: (jnp.maximum(i - steps // 2, 0), 0)
    )
    sent_spec = lambda columns: pl.BlockSpec(
        (block, columns), lambda i, u: (jnp.minimum(i, steps // 2 - 1), 0)
    )
    fixed = lambda rows, columns: pl.BlockSpec((rows, columns), lambda i, u: (0, 0))
    still = lambda value: pl.BlockSpec(
        value.shape, lambda i, u: (0,) * value.ndim, pipeline_mode=pl.Buffered(1)
    )
    halves = [sds((tokens // 2, model), bf16)] * 2
    gate_bf, mix, normed_out, sent, kept, gate_sums = pl.pallas_call(
        middle_kernel,
        grid_spec=pltpu.PrefetchScalarGridSpec(
            num_scalar_prefetch=1,
            grid=(steps,),
            in_specs=[turned(width)] * 4
            + [pl.BlockSpec((block // T, 2, T), lambda i, u: (turn(i, u), 0, 0))]
            + [still(skip), still(gain), still(out_proj)],
            out_specs=[turned(width)] * 3
            + [sent_spec(model), kept_spec(model), fixed(16, width)],
        ),
        out_shape=[sds((tokens, width), bf16)] * 3 + halves + [sds((16, width), f32)],
        name="middle",
    )(upper, gate_raw, grad_normed_out, y, act, scales, skip, gain, out_proj)
    grad_out_proj = dot_tn(normed_out, grad_out).astype(bf16)
    grad_gate_proj = dot_tn(normed, gate_bf).astype(bf16)
    grad_out_proj = lax.psum(grad_out_proj, "dp")
    grad_out_proj = grad_out_proj.astype(f32)
    grad_gate_proj = reduce_rows(grad_gate_proj, "dp", n_dp, f32)

    start = lax.axis_index("tensor") * (tokens // n_tensor)
    own = lambda v: lax.dynamic_slice_in_dim(v, start, tokens // n_tensor, 0)
    if n_tensor == 4:
        block_out = sum_quarters(kept, sent, (tokens_in,), (), block_kernel)
        block_out = gather_rows(block_out, "tensor", n_tensor, bf16, mixed=True)
    else:
        branch = scatter_halves(kept, sent, "tensor", n_tensor)
        block_out = (own(tokens_in).astype(f32) + branch).astype(bf16)
        block_out = lax.all_gather(block_out, "tensor", axis=0, tiled=True)

    consts = (conv_value, conv_state, head_pair, skip)
    given = (mix, y, act, pre, vs_raw, z_raw, sin, aux)
    out = [sds((tokens, full), bf16), sds((8 * (K + 2), wide), f32)]

    def of(value):
        row = lambda i, j: i * per_seq + per_seq - 1 - j
        if len(value.shape) == 2:
            return pl.BlockSpec((T, value.shape[1]), lambda i, j: (row(i, j), 0))
        return pl.BlockSpec((1,) + value.shape[1:], lambda i, j: (row(i, j), 0, 0))

    def whole(value):
        return pl.BlockSpec(value.shape, lambda i, j: (0, 0), pipeline_mode=pl.Buffered(1))

    packed, csum = pl.pallas_call(
        backward_kernel,
        grid=(seqs, per_seq),
        in_specs=[of(v) for v in given] + [whole(v) for v in consts],
        out_specs=[of(out[0]), pl.BlockSpec(out[1].shape, lambda i, j: (0, 0))],
        out_shape=out,
        scratch_shapes=[
            pltpu.VMEM((N, width), f32), pltpu.VMEM((T + 8, wide), f32),
            pltpu.VMEM((3 * T, width), f32), pltpu.VMEM((T, width), bf16),
            pltpu.VMEM((T, width), bf16), pltpu.VMEM((8, LANES), f32),
            pltpu.VMEM((8, LANES), f32), pltpu.VMEM((5, T, width), bf16),
            pltpu.VMEM((LANES, width), bf16), pltpu.VMEM((width, LANES), bf16),
        ],
        name="ssd_backward",
    )(*given, *consts)

    grad_packed = dot_tn(normed, packed).astype(bf16)
    grad_value_proj = grad_packed[:, :width]
    grad_state_proj = grad_packed[:, width:wide]
    grad_step_proj = grad_packed[:, wide : wide + heads].T
    sent, kept, gain_part = pl.pallas_call(
        group_kernel,
        grid_spec=pltpu.PrefetchScalarGridSpec(
            num_scalar_prefetch=1,
            grid=(steps,),
            in_specs=[turned(width), turned(full), turned(model)]
            + [still(w) for w in projections],
            out_specs=[sent_spec(model), kept_spec(model), fixed(8, model)],
            scratch_shapes=[pltpu.VMEM((block, model), bf16)],
        ),
        out_shape=halves + [sds((8, model), f32)],
        name="group_in",
    )(upper, gate_bf, packed, normed, *projections)
    gate_sums = jnp.pad(gate_sums, ((0, 0), (0, 2 * N)))
    sums = jnp.sum(jnp.concatenate([csum, gate_sums]).reshape(K + 4, 8, wide), axis=1)
    gain_part = jnp.sum(gain_part, axis=0) / pre_gain

    grad_value_proj = reduce_rows(grad_value_proj, "dp", n_dp, f32)

    if n_tensor == 4:
        gain_row = pre_gain[None, :]
        grad_in = sum_quarters(kept, sent, (tokens_in, grad_out), (gain_row,), input_kernel)
    else:
        grad_normed = scatter_halves(kept, sent, "tensor", n_tensor)
        own_hidden = own(tokens_in).astype(f32)
        own_inv = lax.rsqrt(jnp.mean(own_hidden * own_hidden, axis=1, keepdims=True) + eps_value)
        weighted = pre_gain * grad_normed
        grad_hidden = own_inv * weighted - own_hidden * (own_inv * own_inv * own_inv) * jnp.mean(
            weighted * own_hidden, axis=1, keepdims=True
        )
        grad_in = (own(grad_out).astype(f32) + grad_hidden).astype(bf16)
    grad_in = lax.all_gather(grad_in, "tensor", axis=0, tiled=True)
    grad_in = copy_rows(grad_in)

    gain_rows = model // (2 * N)
    extra = jnp.concatenate([sums[:, width:], gain_part.reshape(gain_rows, 2 * N)], axis=0)
    unit = n_tensor * math.lcm(16, model // math.gcd(model, 2 * N))
    gap = -(model + extra.shape[0]) % unit
    extra = jnp.pad(extra, ((0, gap), (0, 0))).astype(bf16)
    shared = jnp.concatenate([grad_state_proj, extra], axis=0)
    shared = scatter_sum(shared, "tensor", n_tensor).astype(bf16)
    small = jnp.concatenate([jnp.pad(sums, ((0, 0), (0, model - wide))), grad_step_proj], axis=0)
    part = shared.shape[0]
    flat = part * 2 * N // model
    both = jnp.concatenate([shared.reshape(flat, model), small.astype(bf16)], axis=0)
    both = butterfly(both, "dp", n_dp)
    shared, small = both[:flat].reshape(part, 2 * N), both[flat:].astype(f32)
    shared = gather_rows(shared, "tensor", n_tensor, bf16)
    grad_state_proj = shared[:model].astype(f32)
    state_sums = shared[model : model + K + 4].astype(f32)
    grad_pre_gain = shared[model + K + 4 : model + K + 4 + gain_rows].reshape(model).astype(f32)
    sums = small[: K + 4]
    grad_step_proj = small[K + 4 :].T
    grad_skip = jnp.sum(sums[K + 3, :width].reshape(heads, head_width), axis=1)
    return (
        block_out,
        grad_in,
        grad_pre_gain,
        grad_gate_proj,
        grad_value_proj,
        grad_state_proj,
        grad_step_proj,
        sums[:K, :width],
        sums[K, :width],
        state_sums[:K],
        state_sums[K],
        sums[K + 1, :heads],
        sums[K + 1, LANES : LANES + heads] * decay_rate,
        grad_skip,
        sums[K + 2, :width],
        grad_out_proj,
    )


def solution(mesh):
    t = P("tensor")
    cols = P(None, "tensor")
    in_specs = (
        P("dp", None), P("dp"), P(), cols, cols, P(), cols, cols, t, P(), P(), t, t, t, t,
        P("tensor", None), P("dp", None),
    )
    out_specs = (
        P("dp", None), P("dp", None), P(), cols, cols, P(), cols, cols, t, P(), P(), t, t, t, t,
        P("tensor", None),
    )
    n_dp, n_tensor = mesh.shape["dp"], mesh.shape["tensor"]

    def body(*args):
        return on_device(*args, n_dp=n_dp, n_tensor=n_tensor)

    return jax.shard_map(body, mesh=mesh, in_specs=in_specs, out_specs=out_specs, check_vma=False)
```
